512 devices in a mesh: dp: 8 (over x, core), seq: 64 (over y, z).
Axes of the slice: x: 4, y: 4, z: 16, core: 2. Of those that a mesh axis runs over, the one named last changes fastest.
Arguments:
- inputs: float32 [8, 8192, 128], P('dp', 'seq'), parts along dimension 0, may hold values from -48 to 48
- trajectory: float32 [8, 8192, 128], P('dp', 'seq'), parts along dimension 0, may hold values from -0.9 to 0.9
- initial_state: float32 [8, 128], P('dp'), parts along dimension 0, may hold values from -0.9 to 0.9
- cotangent: float32 [8, 8192, 128], P('dp', 'seq'), parts along dimension 0, may hold values from -1 to 1
- in_weight: float32 [128, 384], replicated, may hold values from -0.5 to 0.5
- recurrent_weight: float32 [128, 384], replicated, may hold values from -0.5 to 0.5
- gate_bias: float32 [384], replicated
Outputs:
- new_state: float32 [8, 8192, 128], P('dp', 'seq'), parts along dimension 0
- adjoint: float32 [8, 8192, 128], P('dp', 'seq'), parts along dimension 0
The draws below stay inside these ranges and needn't reach their ends.
There are 8 independent parts, one for each index of `dp`. The reference program is written for one: setup_inputs(seed, part) draws one part's arguments, and reference() takes and returns one part's arrays. A program takes and returns all parts, laid end to end along the dimension named above; an argument that names none is the same for every part. Nothing has to cross between parts.
All inputs are finite; a program needn't handle non-finite values.
Results may differ from the reference program's by a relative error of at most 0.0003.
Values sent between devices are 32-bit elements; how exact they have to be, the bound alone decides.
No kernel may reach another device: no remote copies, remote signals or barrier semaphores. Data moves between devices by JAX's collectives and lax.ppermute only.
A program may use at most 64 MiB of HBM per device.

```python
import math
import jax
import jax.numpy as jnp
from jax import lax

H = 128
D_IN = 128
TOKENS = 8192


def draw_inputs(key, part):
    first_key, second_key = jax.random.split(key, 2)
    shape = (1, TOKENS, D_IN)
    starting_level = jnp.clip(jax.random.normal(first_key, shape, jnp.float32), -4.0, 4.0)
    picked_locations = jax.random.randint(second_key, (4,), 0, TOKENS)
    linear_map_lines = lax.broadcasted_iota(jnp.int32, (1, TOKENS, 1), 1)
    contiguous_span = jnp.any(linear_map_lines == picked_locations, axis=-1, keepdims=True)
    weighted_summand = starting_level * jnp.where(contiguous_span, 12.0, 1.0)
    return weighted_summand.astype(jnp.float32)


def draw_cotangent(key, part):
    shape = (1, TOKENS, H)
    factor = 2.0 / math.sqrt(TOKENS)
    starting_level = jnp.clip(jax.random.normal(key, shape, jnp.float32), -4.0, 4.0)
    return (starting_level * factor).astype(jnp.float32)


def draw_gate_bias(key, part):
    first_key, second_key, third_key, fourth_key = jax.random.split(key, 4)
    shuffled = jax.random.permutation(first_key, H)
    slow_count = H // 2
    slow_rows = shuffled < slow_count
    slow_bias = -(math.log(TOKENS) + 1.5) + jax.random.uniform(second_key, (H,), jnp.float32, -0.5, 0.5)
    fast_bias = -jax.random.uniform(third_key, (H,), jnp.float32, math.log(30.0), math.log(50.0))
    write_bias = jnp.where(slow_rows, slow_bias, fast_bias)
    others = jax.random.uniform(fourth_key, (2, H), jnp.float32, -1.0, 1.0)
    return jnp.concatenate([others[0], write_bias, others[1]]).astype(jnp.float32)


def steps_of(own_key, dims, cuts, smallest, largest):
    def one(axis_at, blocks):
        heights = jax.random.uniform(jax.random.fold_in(jax.random.fold_in(own_key, 6), axis_at), (blocks,), jnp.float32, smallest / len(cuts), largest / len(cuts))
        return jnp.repeat(jnp.exp(heights), dims[axis_at] // blocks).reshape((-1,) + (1,) * (len(dims) - axis_at - 1))

    gain = one(*cuts[0])
    for cut in cuts[1:]:
        gain = gain * one(*cut)
    return gain


def scatter_about(own_key, shape, deviation, reach, held_as=jnp.bfloat16):
    return jnp.clip(deviation * jax.random.normal(own_key, shape, jnp.float32), -reach, reach).astype(held_as)


def setup_inputs(seed: int = 0, part: int = 0) -> dict:
    key_of = jax.random.split(jax.random.key(seed), 8)
    part_splits = jax.random.split(jax.random.fold_in(key_of[7], part), 8)
    inputs = draw_inputs(jax.random.fold_in(jax.random.fold_in(key_of[7], part), 71), part)
    trajectory = jnp.clip(jax.random.uniform(part_splits[1], (1, TOKENS, H), jnp.float32, -0.9, 0.9) * steps_of(part_splits[1], (1, TOKENS, H), ((1, 64),), -0.4, 0.0), -0.9, 0.9)
    initial_state = jnp.clip(jax.random.uniform(part_splits[2], (1, H), jnp.float32, -0.9, 0.9), -0.9, 0.9)
    cotangent = draw_cotangent(jax.random.fold_in(jax.random.fold_in(key_of[7], part), 71), part)
    in_weight = scatter_about(key_of[4], (D_IN, 3 * H), D_IN ** -0.5, 0.5, jnp.float32)
    recurrent_weight = scatter_about(key_of[5], (H, 3 * H), H ** -0.5, 0.5, jnp.float32)
    gate_bias = draw_gate_bias(jax.random.fold_in(key_of[7], 71), part)
    return dict(inputs=inputs, trajectory=trajectory, initial_state=initial_state, cotangent=cotangent, in_weight=in_weight, recurrent_weight=recurrent_weight, gate_bias=gate_bias)


HIGHEST_PRECISION = lax.Precision.HIGHEST


def sum_parts(tensor, hidden_width):
    return tensor[..., :hidden_width] + tensor[..., hidden_width:2 * hidden_width] + tensor[..., 2 * hidden_width:]


def linearize(features, previous, in_weight, recurrent_weight, gate_bias):
    hidden_width = previous.shape[-1]
    projected = jnp.dot(features, in_weight, precision=HIGHEST_PRECISION, preferred_element_type=jnp.float32) + gate_bias
    recurrent = jnp.dot(previous, recurrent_weight, precision=HIGHEST_PRECISION, preferred_element_type=jnp.float32)
    reset_gate = jax.nn.sigmoid(projected[:, :hidden_width] + recurrent[:, :hidden_width])
    write_gate = jax.nn.sigmoid(projected[:, hidden_width:2 * hidden_width] + recurrent[:, hidden_width:2 * hidden_width])
    cand_recurrent = recurrent[:, 2 * hidden_width:]
    candidate = jnp.tanh(projected[:, 2 * hidden_width:] + reset_gate * cand_recurrent)
    updated = previous + write_gate * (candidate - previous)
    keep_rate = 1.0 - write_gate
    slopes = write_gate * (1.0 - candidate * candidate)
    gate_terms = jnp.concatenate([slopes * cand_recurrent * reset_gate * (1.0 - reset_gate), (candidate - previous) * write_gate * (1.0 - write_gate), slopes * reset_gate], axis=1)
    offsets = updated - keep_rate * previous - sum_parts(gate_terms * recurrent, hidden_width)
    return keep_rate, gate_terms, offsets


def apply_jacobian(keep_rate, gate_terms, vector, recurrent_weight):
    hidden_width = vector.shape[-1]
    mapped = jnp.einsum('bk,kj->bj', vector, recurrent_weight, precision=HIGHEST_PRECISION)
    return keep_rate * vector + sum_parts(gate_terms * mapped, hidden_width)


def apply_transposed(keep_rate, gate_terms, vector, recurrent_weight):
    tiled = jnp.concatenate([vector, vector, vector], axis=-1)
    return keep_rate * vector + jnp.einsum('bk,jk->bj', gate_terms * tiled, recurrent_weight, precision=HIGHEST_PRECISION)


def reference(inputs, trajectory, initial_state, cotangent, in_weight, recurrent_weight, gate_bias):
    path = trajectory[0]
    previous = jnp.concatenate([initial_state, path[:-1]], axis=0)
    keep_rate, gate_terms, offsets = linearize(inputs[0], previous, in_weight, recurrent_weight, gate_bias)

    def forward(hidden_state, step_items):
        keep_now, terms_now, offset_now = step_items
        hidden_state = apply_jacobian(keep_now[None], terms_now[None], hidden_state[None], recurrent_weight)[0] + offset_now
        return hidden_state, hidden_state

    _, states = lax.scan(forward, initial_state[0], (keep_rate, gate_terms, offsets))

    def backward(carried, step_items):
        keep_now, terms_now, cotan_now = step_items
        costate = cotan_now + carried
        carried = apply_transposed(keep_now[None], terms_now[None], costate[None], recurrent_weight)[0]
        return carried, costate

    start_adjoint = jnp.zeros((path.shape[1],), jnp.float32)
    _, adjoint_rows = lax.scan(backward, start_adjoint, (keep_rate, gate_terms, cotangent[0]), reverse=True)
    return states[None], adjoint_rows[None]
```

```python
import jax
import jax.numpy as jnp
from jax import lax
from jax.experimental import pallas as pl
from jax.experimental.pallas import tpu as pltpu
from jax.sharding import PartitionSpec as P

F32 = jnp.float32
BF16 = jnp.bfloat16
H = 128
BLOCKS = 16
ROW_B = 128
ROW_C = 129
ROW_PROJ = 130
ROW_REC = 133
ROW_LAST = 136
ROWS = 144
VMEM_LIMIT = 48 * 1024 * 1024


def split(x):
    hi = x.astype(BF16)
    return hi, (x - hi.astype(F32)).astype(BF16)


def left(x):
    return jnp.concatenate(split(x), axis=1)


def right(x):
    row = jnp.concatenate(split(x), axis=1)
    return jnp.concatenate([row, row], axis=0)


def right_t(x):
    hi, lo = split(x)
    return jnp.concatenate(
        [jnp.concatenate([hi, hi], axis=1), jnp.concatenate([lo, lo], axis=1)], axis=0
    )


def both_halves(out):
    half = out.shape[1] // 2
    return out[:, :half] + out[:, half:]


def mm(a, b):
    return both_halves(jnp.dot(left(a), right(b), preferred_element_type=F32))


def mm_t(a, b):
    return both_halves(
        lax.dot_general(
            left(a), right_t(b), (((1,), (1,)), ((), ())), preferred_element_type=F32
        )
    )


def pad8(row):
    return jnp.broadcast_to(row, (8, H))


def vec_mm(row, b):
    return mm(pad8(row), b)[:1]


def vec_mm_t(row, b):
    return mm_t(pad8(row), b)[:1]


def eye():
    rows = lax.broadcasted_iota(jnp.int32, (H, H), 0)
    cols = lax.broadcasted_iota(jnp.int32, (H, H), 1)
    return (rows == cols).astype(F32)


def gates(proj, rec, prev):
    reset = jax.nn.sigmoid(proj[0] + rec[0])
    write = jax.nn.sigmoid(proj[1] + rec[1])
    cand = jnp.tanh(proj[2] + reset * rec[2])
    slope = write * (1.0 - cand * cand)
    terms = (
        slope * rec[2] * reset * (1.0 - reset),
        (cand - prev) * write * (1.0 - write),
        slope * reset,
    )
    off = write * cand - (terms[0] * rec[0] + terms[1] * rec[1] + terms[2] * rec[2])
    return write, terms, off


def parts3(x):
    return x[:, :H], x[:, H : 2 * H], x[:, 2 * H :]


def leaf(u, write, terms, ident):
    return u[0] * terms[0] + u[1] * terms[1] + u[2] * terms[2] - ident * write


def compose(early, late):
    lb, lv, lc = early
    rb, rv, rc = late
    prod = mm(jnp.concatenate([lb, pad8(lv)], axis=0), rb)
    return (
        lb + rb + prod[:H],
        lv + rv + prod[H : H + 1],
        lc + rc + vec_mm_t(rc, lb),
    )


def local_kernel(
    x_ref,
    traj_ref,
    cot_ref,
    init_ref,
    win_ref,
    wrec_ref,
    bias_ref,
    pack_ref,
    nodes_ref,
    vecs_ref,
    steps_ref,
    recinit_ref,
):
    traj = traj_ref[0]
    proj = (
        jnp.dot(x_ref[0], win_ref[...], precision=lax.Precision.HIGHEST, preferred_element_type=F32)
        + bias_ref[...]
    )
    rec_in = jnp.concatenate([traj, pad8(init_ref[...])], axis=0)
    rec_all = jnp.dot(
        rec_in, wrec_ref[...], precision=lax.Precision.HIGHEST, preferred_element_type=F32
    )
    recinit_ref[...] = rec_all[H : H + 1]
    rec_rows = rec_all[:H]
    rec = pltpu.roll(rec_rows, 1, 0)
    prev = pltpu.roll(traj, 1, 0)
    write, terms, off = gates(parts3(proj), parts3(rec), prev)
    inner = lax.broadcasted_iota(jnp.int32, (H, H), 0) > 0
    write = jnp.where(inner, write, 0.0)
    terms = [jnp.where(inner, t, 0.0) for t in terms]
    off = jnp.where(inner, off, 0.0)
    for p, rows in enumerate((*terms, write, off)):
        steps_ref[p] = rows

    ident = eye()
    per_block = H // BLOCKS

    def one_block(k, carry):
        base = pl.multiple_of(k * per_block, per_block)
        rows = [steps_ref[p, pl.ds(base, per_block), :] for p in range(4)]
        u = [wrec_ref[:, p * H : (p + 1) * H] for p in range(3)]
        maps = []
        for l in range(per_block):
            row = [r[l : l + 1] for r in rows]
            maps.append(leaf(u, row[3], row[:3], ident))
        while len(maps) > 1:
            maps = [
                maps[i] + maps[i + 1] + mm(maps[i], maps[i + 1]) for i in range(0, len(maps), 2)
            ]
        nodes_ref[BLOCKS + k] = maps[0]
        return carry

    lax.fori_loop(0, BLOCKS, one_block, 0)

    u_right, u_right_t = weights_of(wrec_ref)
    fwd = jnp.zeros((BLOCKS, H), F32)
    bwd = jnp.zeros((BLOCKS, H), F32)
    for l in range(per_block):
        fwd = forward_step(fwd, steps_ref, l, u_right, per_block)
        _, bwd = backward_step(bwd, steps_ref, cot_ref, per_block - 1 - l, u_right_t, per_block)
    vecs_ref[BLOCKS : 2 * BLOCKS, :H] = fwd
    vecs_ref[BLOCKS : 2 * BLOCKS, H:] = bwd

    def node(n):
        return nodes_ref[n], vecs_ref[n : n + 1, :H], vecs_ref[n : n + 1, H:]

    for n in range(BLOCKS - 1, 0, -1):
        m, v, c = compose(node(2 * n), node(2 * n + 1))
        nodes_ref[n] = m
        vecs_ref[n : n + 1, :H] = v
        vecs_ref[n : n + 1, H:] = c
    nodes_ref[0] = jnp.zeros((H, H), F32)
    vecs_ref[0:1, :] = jnp.zeros((1, 2 * H), F32)
    m, v, c = node(1)
    rec_last = rec_rows[H - 1 : H]
    write_pack(
        pack_ref,
        m,
        [v, c]
        + [proj[0:1, p * H : (p + 1) * H] for p in range(3)]
        + [rec_last[:, p * H : (p + 1) * H] for p in range(3)]
        + [traj[H - 1 : H]],
    )


def write_pack(pack_ref, m, rows):
    tail = jnp.concatenate(rows + [jnp.zeros((ROWS - H - len(rows), H), F32)], axis=0)
    for i in range(pack_ref.shape[0]):
        pack_ref[i, :H] = m
        pack_ref[i, H:] = tail


def weights_of(wrec_ref):
    u = wrec_ref[...]
    return right(u), right_t(u)


def every(ref, l, per_block):
    return ref[pl.ds(l, BLOCKS, stride=per_block), :]


def forward_step(h, steps_ref, l, u_right, per_block):
    term = [every(steps_ref.at[p], l, per_block) for p in range(5)]
    mapped = parts3(both_halves(jnp.dot(left(h), u_right, preferred_element_type=F32)))
    moved = term[0] * mapped[0] + term[1] * mapped[1] + term[2] * mapped[2]
    return h + (moved - term[3] * h) + term[4]


def backward_step(carried, steps_ref, cot_ref, l, u_right_t, per_block):
    term = [every(steps_ref.at[p], l, per_block) for p in range(4)]
    costate = carried + every(cot_ref.at[0], l, per_block)
    scaled = jnp.concatenate([term[p] * costate for p in range(3)], axis=1)
    back = both_halves(
        lax.dot_general(
            left(scaled), u_right_t, (((1,), (1,)), ((), ())), preferred_element_type=F32
        )
    )
    return costate, costate + (back - term[3] * costate)


def boundaries(group_ref, wrec_ref, ident):
    u = [wrec_ref[:, p * H : (p + 1) * H] for p in range(3)]
    found = []
    for j in range(1, 4):
        proj = [group_ref[j, ROW_PROJ + p : ROW_PROJ + p + 1] for p in range(3)]
        rec = [group_ref[j - 1, ROW_REC + p : ROW_REC + p + 1] for p in range(3)]
        write, terms, off = gates(proj, rec, group_ref[j - 1, ROW_LAST : ROW_LAST + 1])
        found.append((leaf(u, write, terms, ident), off))
    return found


def links(group_ref, wrec_ref):
    ident = eye()
    firsts = boundaries(group_ref, wrec_ref, ident)
    ahead, behind = [], []
    for j in range(3):
        first, off = firsts[j]
        part = group_ref[j, :H]
        prod = mm(group_ref[j, : H + 8], first)
        ahead.append(
            (
                part + first + prod[:H],
                group_ref[j, ROW_B : ROW_B + 1] + off + prod[ROW_B : ROW_B + 1],
            )
        )
        part = group_ref[j + 1, :H]
        cc = group_ref[j + 1, ROW_C : ROW_C + 1]
        prod = mm(jnp.concatenate([first, pad8(off)], axis=0), part)
        behind.append(
            (
                part + first + prod[:H],
                off + prod[H : H + 1] + group_ref[j + 1, ROW_B : ROW_B + 1],
                cc + vec_mm_t(cc, first),
            )
        )
    return ahead, behind


def merge_kernel(group_ref, wrec_ref, pack_ref, ahead_ref, behind_ref):
    ahead, behind = links(group_ref, wrec_ref)
    for j in range(3):
        m, v = ahead[j]
        ahead_ref[j, :H] = m
        ahead_ref[j, H:] = pad8(v)
        m, v, c = behind[j]
        behind_ref[j, :H] = m
        behind_ref[j, H:] = pad8(c)
    start = (
        group_ref[0, :H],
        group_ref[0, ROW_B : ROW_B + 1],
        group_ref[0, ROW_C : ROW_C + 1],
    )
    m, v, c = compose(compose(start, behind[0]), compose(behind[1], behind[2]))
    write_pack(
        pack_ref,
        m,
        [v, c]
        + [group_ref[0, ROW_PROJ + p : ROW_PROJ + p + 1] for p in range(3)]
        + [group_ref[3, ROW_REC + p : ROW_REC + p + 1] for p in range(3)]
        + [group_ref[3, ROW_LAST : ROW_LAST + 1]],
    )


def apply_kernel(
    place_ref,
    group_ref,
    ahead2_ref,
    behind2_ref,
    ahead1_ref,
    behind1_ref,
    nodes_ref,
    vecs_ref,
    steps_ref,
    cot_ref,
    init_ref,
    recinit_ref,
    wrec_ref,
    state_ref,
    adjoint_ref,
):
    per_block = H // BLOCKS
    ahead3, behind3 = links(group_ref, wrec_ref)
    u_right, u_right_t = weights_of(wrec_ref)
    init = init_ref[...]
    rec = recinit_ref[...]
    write, terms, off = gates(
        [group_ref[0, ROW_PROJ + p : ROW_PROJ + p + 1] for p in range(3)], parts3(rec), init
    )
    state = (
        init
        + (terms[0] * rec[:, :H] + terms[1] * rec[:, H : 2 * H] + terms[2] * rec[:, 2 * H :])
        - write * init
        + off
    )
    costate = jnp.zeros((1, H), F32)

    levels = [
        ([a[0] for a in ahead3], [a[1] for a in ahead3], [b[0] for b in behind3], [b[2] for b in behind3])
    ]
    for ahead_ref, behind_ref in ((ahead2_ref, behind2_ref), (ahead1_ref, behind1_ref)):
        levels.append(
            (
                [ahead_ref[j, :H] for j in range(3)],
                [ahead_ref[j, H : H + 1] for j in range(3)],
                [behind_ref[j, :H] for j in range(3)],
                [behind_ref[j, H : H + 1] for j in range(3)],
            )
        )
    for level, (fm, fv, bm, bv) in enumerate(levels):
        own = place_ref[level]
        for j in range(3):
            moved = state + vec_mm(state, fm[j]) + fv[j]
            state = jnp.where(j < own, moved, state)
            i = 2 - j
            moved = costate + vec_mm_t(costate, bm[i]) + bv[i]
            costate = jnp.where(i >= own, moved, costate)

    states = {1: state}
    costates = {1: costate}
    for n in range(1, BLOCKS):
        states[2 * n] = states[n]
        states[2 * n + 1] = (
            states[n] + vec_mm(states[n], nodes_ref[2 * n]) + vecs_ref[2 * n : 2 * n + 1, :H]
        )
        costates[2 * n + 1] = costates[n]
        costates[2 * n] = (
            costates[n]
            + vec_mm_t(costates[n], nodes_ref[2 * n + 1])
            + vecs_ref[2 * n + 1 : 2 * n + 2, H:]
        )
    fwd = jnp.concatenate([states[BLOCKS + k] for k in range(BLOCKS)], axis=0)
    bwd = jnp.concatenate([costates[BLOCKS + k] for k in range(BLOCKS)], axis=0)
    for l in range(per_block):
        fwd = forward_step(fwd, steps_ref, l, u_right, per_block)
        state_ref.at[0][pl.ds(l, BLOCKS, stride=per_block), :] = fwd
        back = per_block - 1 - l
        out, bwd = backward_step(bwd, steps_ref, cot_ref, back, u_right_t, per_block)
        adjoint_ref.at[0][pl.ds(back, BLOCKS, stride=per_block), :] = out


def call(kernel, out_shape, flops, count, scalars=0):
    vmem = pl.BlockSpec(memory_space=pltpu.VMEM)
    smem = pl.BlockSpec(memory_space=pltpu.SMEM)
    return pl.pallas_call(
        kernel,
        out_shape=out_shape,
        in_specs=[smem] * scalars + [vmem] * (count - scalars),
        out_specs=tuple(vmem for _ in out_shape),
        compiler_params=pltpu.CompilerParams(vmem_limit_bytes=VMEM_LIMIT),
        cost_estimate=pl.CostEstimate(flops=flops, bytes_accessed=2**20, transcendentals=0),
    )


def group_lists(count):
    near = [list(range(s, s + 4)) for s in range(0, count, 4)]
    middle = [
        [16 * y + i, 16 * y + 4 + i, 16 * y + 11 - i, 16 * y + 15 - i]
        for y in range(count // 16)
        for i in range(4)
    ]
    far = [[16 * y + z for y in range(4)] for z in range(16)]
    return near, middle, far


def shape(*dims):
    return jax.ShapeDtypeStruct(dims, F32)


def per_device(
    inputs, trajectory, initial_state, cotangent, in_weight, recurrent_weight, gate_bias
):
    near, middle, far = group_lists(lax.axis_size("seq"))
    place = lax.axis_index("seq")
    places = jnp.stack([place // 16, place // 4 % 4, place % 4]).astype(jnp.int32)
    pack, nodes, vecs, steps, recinit = call(
        local_kernel,
        (
            shape(4, ROWS, H),
            shape(2 * BLOCKS, H, H),
            shape(2 * BLOCKS, 2 * H),
            shape(5, H, H),
            shape(1, 3 * H),
        ),
        2 * 10**9,
        7,
    )(
        inputs,
        trajectory,
        cotangent,
        initial_state,
        in_weight,
        recurrent_weight,
        gate_bias.reshape(1, -1),
    )
    merge = call(
        merge_kernel, (shape(4, ROWS, H), shape(3, H + 8, H), shape(3, H + 8, H)), 10**8, 2
    )

    def exchange(packed, groups):
        return lax.all_to_all(packed, "seq", 0, 0, axis_index_groups=groups)

    pack, ahead1, behind1 = merge(exchange(pack, near), recurrent_weight)
    pack, ahead2, behind2 = merge(exchange(pack, middle), recurrent_weight)
    group = exchange(pack, far)
    new_state, adjoint = call(apply_kernel, (shape(1, H, H), shape(1, H, H)), 10**8, 13, 1)(
        places,
        group,
        ahead2,
        behind2,
        ahead1,
        behind1,
        nodes,
        vecs,
        steps,
        cotangent,
        initial_state,
        recinit,
        recurrent_weight,
    )
    return new_state, adjoint


def solution(mesh):
    return jax.shard_map(
        per_device,
        mesh=mesh,
        in_specs=(
            P("dp", "seq", None),
            P("dp", "seq", None),
            P("dp", None),
            P("dp", "seq", None),
            P(),
            P(),
            P(),
        ),
        out_specs=(P("dp", "seq", None), P("dp", "seq", None)),
        check_vma=False,
    )
```

```python
import jax
import jax.numpy as jnp
from jax import lax
from jax.experimental import pallas as pl
from jax.experimental.pallas import tpu as pltpu
from jax.sharding import PartitionSpec as P

F32 = jnp.float32
BF16 = jnp.bfloat16
H = 128
BLOCKS = 16
ROW_B = 128
ROW_C = 129
ROW_PROJ = 130
ROW_REC = 133
ROW_LAST = 136
ROWS = 144
VMEM_LIMIT = 24 * 1024 * 1024


def split(x):
    hi = x.astype(BF16)
    return hi, (x - hi.astype(F32)).astype(BF16)


def left(x):
    return jnp.concatenate(split(x), axis=1)


def right(x):
    row = jnp.concatenate(split(x), axis=1)
    return jnp.concatenate([row, row], axis=0)


def right_t(x):
    hi, lo = split(x)
    return jnp.concatenate(
        [jnp.concatenate([hi, hi], axis=1), jnp.concatenate([lo, lo], axis=1)], axis=0
    )


def both_halves(out):
    half = out.shape[1] // 2
    return out[:, :half] + out[:, half:]


def mm(a, b):
    return both_halves(jnp.dot(left(a), right(b), preferred_element_type=F32))


def mm_t(a, b):
    return both_halves(
        lax.dot_general(
            left(a), right_t(b), (((1,), (1,)), ((), ())), preferred_element_type=F32
        )
    )


def pad8(row):
    return jnp.broadcast_to(row, (8, H))


def vec_mm(row, b):
    return mm(pad8(row), b)[:1]


def vec_mm_t(row, b):
    return mm_t(pad8(row), b)[:1]


def eye():
    rows = lax.broadcasted_iota(jnp.int32, (H, H), 0)
    cols = lax.broadcasted_iota(jnp.int32, (H, H), 1)
    return (rows == cols).astype(F32)


def gates(proj, rec, prev):
    reset = jax.nn.sigmoid(proj[0] + rec[0])
    write = jax.nn.sigmoid(proj[1] + rec[1])
    cand = jnp.tanh(proj[2] + reset * rec[2])
    slope = write * (1.0 - cand * cand)
    terms = (
        slope * rec[2] * reset * (1.0 - reset),
        (cand - prev) * write * (1.0 - write),
        slope * reset,
    )
    off = write * cand - (terms[0] * rec[0] + terms[1] * rec[1] + terms[2] * rec[2])
    return write, terms, off


def parts3(x):
    return x[:, :H], x[:, H : 2 * H], x[:, 2 * H :]


def leaf(u, write, terms, ident):
    return u[0] * terms[0] + u[1] * terms[1] + u[2] * terms[2] - ident * write


def compose(early, late):
    lb, lv, lc = early
    rb, rv, rc = late
    prod = mm(jnp.concatenate([lb, pad8(lv)], axis=0), rb)
    return (
        lb + rb + prod[:H],
        lv + rv + prod[H : H + 1],
        lc + rc + vec_mm_t(rc, lb),
    )


def local_kernel(
    x_hbm,
    traj_hbm,
    cot_hbm,
    init_hbm,
    win_hbm,
    wrec_hbm,
    bias_hbm,
    pack_ref,
    nodes_ref,
    steps_hbm,
    x_ref,
    traj_ref,
    cot_ref,
    init_ref,
    win_ref,
    wrec_ref,
    bias_ref,
    steps_ref,
    pairs_ref,
    quads_ref,
    sems,
):
    copies = [
        pltpu.make_async_copy(src, dst, sems.at[i])
        for i, (src, dst) in enumerate(
            (
                (traj_hbm, traj_ref),
                (wrec_hbm, wrec_ref),
                (init_hbm, init_ref),
                (x_hbm, x_ref),
                (win_hbm, win_ref),
                (bias_hbm, bias_ref),
                (cot_hbm, cot_ref),
            )
        )
    ]
    for copy in copies:
        copy.start()
    for copy in copies[:3]:
        copy.wait()
    traj = traj_ref[0]
    rec_in = jnp.concatenate([traj, pad8(init_ref[...])], axis=0)
    rec_all = jnp.dot(
        rec_in, wrec_ref[...], precision=lax.Precision.HIGHEST, preferred_element_type=F32
    )
    rec_init = rec_all[H : H + 1]
    rec_rows = rec_all[:H]
    for copy in copies[3:]:
        copy.wait()
    proj = (
        jnp.dot(x_ref[0], win_ref[...], precision=lax.Precision.HIGHEST, preferred_element_type=F32)
        + bias_ref[...].reshape(1, 3 * H)
    )
    rec = pltpu.roll(rec_rows, 1, 0)
    prev = pltpu.roll(traj, 1, 0)
    write, terms, off = gates(parts3(proj), parts3(rec), prev)
    inner = lax.broadcasted_iota(jnp.int32, (H, H), 0) > 0
    write = jnp.where(inner, write, 0.0)
    terms = [jnp.where(inner, t, 0.0) for t in terms]
    off = jnp.where(inner, off, 0.0)
    for p, rows in enumerate((*terms, write, off)):
        steps_ref[p] = rows
    save = pltpu.make_async_copy(steps_ref, steps_hbm, sems.at[7])
    save.start()

    ident = eye()
    per_block = H // BLOCKS
    u_right, u_right_t = weights_of(wrec_ref)

    def some_pairs(k, carry):
        fwd, bwd = carry
        base = pl.multiple_of(k * 16, 16)
        for half in range(2):
            rows = [steps_ref[p, pl.ds(base + 8 * half, 8), :] for p in range(4)]
            u = [wrec_ref[:, p * H : (p + 1) * H] for p in range(3)]
            for i in range(4):
                maps = []
                for l in (2 * i, 2 * i + 1):
                    row = [r[l : l + 1] for r in rows]
                    maps.append(leaf(u, row[3], row[:3], ident))
                pairs_ref[8 * k + 4 * half + i] = maps[0] + maps[1] + mm(*maps)
        fwd = forward_step(fwd, steps_ref, k, u_right, per_block)
        _, bwd = backward_step(bwd, steps_ref, cot_ref, per_block - 1 - k, u_right_t, per_block)
        return fwd, bwd

    zero = jnp.zeros((BLOCKS, H), F32)
    fwd, bwd = lax.fori_loop(0, 8, some_pairs, (zero, zero))
    for k in range(BLOCKS):
        nodes_ref[BLOCKS + k, H:] = two_rows(fwd[k : k + 1], bwd[k : k + 1])

    def joined(ref, i):
        early, late = ref[2 * i], ref[2 * i + 1]
        return early + late + mm(early, late)

    def some_quads(k, carry):
        for i in range(8):
            quads_ref[8 * k + i] = joined(pairs_ref, 8 * k + i)
        return carry

    lax.fori_loop(0, 4, some_quads, 0)

    def some_blocks(k, carry):
        for i in range(8):
            nodes_ref[BLOCKS + 8 * k + i, :H] = joined(quads_ref, 8 * k + i)
        return carry

    lax.fori_loop(0, 2, some_blocks, 0)

    def node(n):
        return nodes_ref[n, :H], nodes_ref[n, H : H + 1], nodes_ref[n, H + 1 : H + 2]

    for n in range(BLOCKS - 1, 0, -1):
        m, v, c = compose(node(2 * n), node(2 * n + 1))
        nodes_ref[n, :H] = m
        nodes_ref[n, H:] = two_rows(v, c)
    nodes_ref[0, :8] = jnp.concatenate([*parts3(rec_init), jnp.zeros((5, H), F32)], axis=0)
    nodes_ref[0, 8:] = jnp.zeros((H, H), F32)
    m, v, c = node(1)
    rec_last = rec_rows[H - 1 : H]
    write_pack(
        pack_ref,
        m,
        [v, c]
        + [proj[0:1, p * H : (p + 1) * H] for p in range(3)]
        + [rec_last[:, p * H : (p + 1) * H] for p in range(3)]
        + [traj[H - 1 : H]],
    )
    save.wait()


def two_rows(v, c):
    return jnp.concatenate([v, c, jnp.zeros((6, H), F32)], axis=0)


def write_pack(pack_ref, m, rows):
    tail = jnp.concatenate(rows + [jnp.zeros((ROWS - H - len(rows), H), F32)], axis=0)
    for i in range(pack_ref.shape[0]):
        pack_ref[i, :H] = m
        pack_ref[i, H:] = tail


def weights_of(wrec_ref):
    u = wrec_ref[...]
    return right(u), right_t(u)


def every(ref, l, per_block):
    return ref[pl.ds(l, BLOCKS, stride=per_block), :]


def forward_step(h, steps_ref, l, u_right, per_block):
    term = [every(steps_ref.at[p], l, per_block) for p in range(5)]
    mapped = parts3(both_halves(jnp.dot(left(h), u_right, preferred_element_type=F32)))
    moved = term[0] * mapped[0] + term[1] * mapped[1] + term[2] * mapped[2]
    return h + (moved - term[3] * h) + term[4]


def backward_step(carried, steps_ref, cot_ref, l, u_right_t, per_block):
    term = [every(steps_ref.at[p], l, per_block) for p in range(4)]
    costate = carried + every(cot_ref.at[0], l, per_block)
    scaled = jnp.concatenate([term[p] * costate for p in range(3)], axis=1)
    back = both_halves(
        lax.dot_general(
            left(scaled), u_right_t, (((1,), (1,)), ((), ())), preferred_element_type=F32
        )
    )
    return costate, costate + (back - term[3] * costate)


def boundaries(group_ref, wrec_ref, ident):
    u = [wrec_ref[:, p * H : (p + 1) * H] for p in range(3)]
    found = []
    for j in range(1, 4):
        proj = [group_ref[j, ROW_PROJ + p : ROW_PROJ + p + 1] for p in range(3)]
        rec = [group_ref[j - 1, ROW_REC + p : ROW_REC + p + 1] for p in range(3)]
        write, terms, off = gates(proj, rec, group_ref[j - 1, ROW_LAST : ROW_LAST + 1])
        found.append((leaf(u, write, terms, ident), off))
    return found


def links(group_ref, wrec_ref):
    ident = eye()
    firsts = boundaries(group_ref, wrec_ref, ident)
    ahead, behind = [], []
    for j in range(3):
        first, off = firsts[j]
        part = group_ref[j, :H]
        prod = mm(group_ref[j, : H + 8], first)
        ahead.append(
            (
                part + first + prod[:H],
                group_ref[j, ROW_B : ROW_B + 1] + off + prod[ROW_B : ROW_B + 1],
            )
        )
        part = group_ref[j + 1, :H]
        cc = group_ref[j + 1, ROW_C : ROW_C + 1]
        prod = mm(jnp.concatenate([first, pad8(off)], axis=0), part)
        behind.append(
            (
                part + first + prod[:H],
                off + prod[H : H + 1] + group_ref[j + 1, ROW_B : ROW_B + 1],
                cc + vec_mm_t(cc, first),
            )
        )
    return ahead, behind


def merge_kernel(group_ref, wrec_ref, pack_ref, links_ref):
    ahead, behind = links(group_ref, wrec_ref)
    for j in range(3):
        m, v = ahead[j]
        links_ref[j, :H] = m
        links_ref[j, H:] = pad8(v)
        m, v, c = behind[j]
        links_ref[3 + j, :H] = m
        links_ref[3 + j, H:] = pad8(c)
    start = (
        group_ref[0, :H],
        group_ref[0, ROW_B : ROW_B + 1],
        group_ref[0, ROW_C : ROW_C + 1],
    )
    m, v, c = compose(compose(start, behind[0]), compose(behind[1], behind[2]))
    write_pack(
        pack_ref,
        m,
        [v, c]
        + [group_ref[0, ROW_PROJ + p : ROW_PROJ + p + 1] for p in range(3)]
        + [group_ref[3, ROW_REC + p : ROW_REC + p + 1] for p in range(3)]
        + [group_ref[3, ROW_LAST : ROW_LAST + 1]],
    )


def apply_kernel(
    group_ref,
    links2_ref,
    links1_ref,
    nodes_ref,
    steps_hbm,
    cot_hbm,
    init_hbm,
    wrec_ref,
    state_ref,
    adjoint_ref,
    steps_ref,
    cot_ref,
    init_ref,
    sems,
):
    copies = [
        pltpu.make_async_copy(init_hbm, init_ref, sems.at[0]),
        pltpu.make_async_copy(steps_hbm, steps_ref, sems.at[1]),
        pltpu.make_async_copy(cot_hbm, cot_ref, sems.at[2]),
    ]
    for copy in copies:
        copy.start()
    per_block = H // BLOCKS
    ahead3, behind3 = links(group_ref, wrec_ref)
    u_right, u_right_t = weights_of(wrec_ref)
    copies[0].wait()
    init = init_ref[...]
    rec = [nodes_ref[0, p : p + 1] for p in range(3)]
    write, terms, off = gates(
        [group_ref[0, ROW_PROJ + p : ROW_PROJ + p + 1] for p in range(3)], rec, init
    )
    state = (
        init
        + (terms[0] * rec[0] + terms[1] * rec[1] + terms[2] * rec[2])
        - write * init
        + off
    )
    costate = jnp.zeros((1, H), F32)

    levels = [
        ([a[0] for a in ahead3], [a[1] for a in ahead3], [b[0] for b in behind3], [b[2] for b in behind3])
    ]
    for links_ref in (links2_ref, links1_ref):
        levels.append(
            (
                [links_ref[j, :H] for j in range(3)],
                [links_ref[j, H : H + 1] for j in range(3)],
                [links_ref[3 + j, :H] for j in range(3)],
                [links_ref[3 + j, H : H + 1] for j in range(3)],
            )
        )
    place = lax.axis_index("seq")
    places = (place // 16, place // 4 % 4, place % 4)
    for level, (fm, fv, bm, bv) in enumerate(levels):
        own = places[level]
        for j in range(3):
            moved = state + vec_mm(state, fm[j]) + fv[j]
            state = jnp.where(j < own, moved, state)
            i = 2 - j
            moved = costate + vec_mm_t(costate, bm[i]) + bv[i]
            costate = jnp.where(i >= own, moved, costate)

    states = {1: state}
    costates = {1: costate}
    for n in range(1, BLOCKS):
        states[2 * n] = states[n]
        states[2 * n + 1] = (
            states[n] + vec_mm(states[n], nodes_ref[2 * n, :H]) + nodes_ref[2 * n, H : H + 1]
        )
        costates[2 * n + 1] = costates[n]
        costates[2 * n] = (
            costates[n]
            + vec_mm_t(costates[n], nodes_ref[2 * n + 1, :H])
            + nodes_ref[2 * n + 1, H + 1 : H + 2]
        )
    fwd = jnp.concatenate([states[BLOCKS + k] for k in range(BLOCKS)], axis=0)
    bwd = jnp.concatenate([costates[BLOCKS + k] for k in range(BLOCKS)], axis=0)
    for copy in copies[1:]:
        copy.wait()
    for l in range(per_block):
        fwd = forward_step(fwd, steps_ref, l, u_right, per_block)
        state_ref.at[0][pl.ds(l, BLOCKS, stride=per_block), :] = fwd
        back = per_block - 1 - l
        out, bwd = backward_step(bwd, steps_ref, cot_ref, back, u_right_t, per_block)
        adjoint_ref.at[0][pl.ds(back, BLOCKS, stride=per_block), :] = out


def call(kernel, out_shape, flops, spaces, outs, scratch=()):
    kinds = {"s": pltpu.SMEM, "v": pltpu.VMEM, "h": pltpu.HBM}
    run = pl.pallas_call(
        kernel,
        out_shape=tuple(
            pltpu.HBM(o.shape, o.dtype) if k == "h" else o for k, o in zip(outs, out_shape)
        ),
        in_specs=[pl.BlockSpec(memory_space=kinds[k]) for k in spaces],
        out_specs=tuple(pl.BlockSpec(memory_space=kinds[k]) for k in outs),
        scratch_shapes=list(scratch),
        compiler_params=pltpu.CompilerParams(vmem_limit_bytes=VMEM_LIMIT),
        cost_estimate=pl.CostEstimate(flops=flops, bytes_accessed=2**20, transcendentals=0),
    )

    def placed(*args):
        return run(
            *(
                pltpu.with_memory_space_constraint(a, pltpu.HBM) if k == "h" else a
                for k, a in zip(spaces, args)
            )
        )

    return placed


def group_lists(count):
    near = [list(range(s, s + 4)) for s in range(0, count, 4)]
    middle = [
        [16 * y + i, 16 * y + 4 + i, 16 * y + 11 - i, 16 * y + 15 - i]
        for y in range(count // 16)
        for i in range(4)
    ]
    far = [[16 * y + z for y in range(4)] for z in range(16)]
    return near, middle, far


def shape(*dims):
    return jax.ShapeDtypeStruct(dims, F32)


def per_device(
    inputs, trajectory, initial_state, cotangent, in_weight, recurrent_weight, gate_bias
):
    near, middle, far = group_lists(lax.axis_size("seq"))
    pack, nodes, steps = call(
        local_kernel,
        (
            shape(4, ROWS, H),
            shape(2 * BLOCKS, H + 8, H),
            shape(5, H, H),
        ),
        2 * 10**9,
        "hhhhhhh",
        "vvh",
        [
            pltpu.VMEM((1, H, H), F32),
            pltpu.VMEM((1, H, H), F32),
            pltpu.VMEM((1, H, H), F32),
            pltpu.VMEM((1, H), F32),
            pltpu.VMEM((H, 3 * H), F32),
            pltpu.VMEM((H, 3 * H), F32),
            pltpu.VMEM((3 * H,), F32),
            pltpu.VMEM((5, H, H), F32),
            pltpu.VMEM((64, H, H), F32),
            pltpu.VMEM((32, H, H), F32),
            pltpu.SemaphoreType.DMA((8,)),
        ],
    )(
        inputs,
        trajectory,
        cotangent,
        initial_state,
        in_weight,
        recurrent_weight,
        gate_bias,
    )
    merge = call(
        merge_kernel, (shape(4, ROWS, H), shape(6, H + 8, H)), 10**8, "vv", "vv"
    )

    def exchange(packed, groups):
        return lax.all_to_all(packed, "seq", 0, 0, axis_index_groups=groups)

    pack, links1 = merge(exchange(pack, near), recurrent_weight)
    pack, links2 = merge(exchange(pack, middle), recurrent_weight)
    group = exchange(pack, far)
    new_state, adjoint = call(
        apply_kernel,
        (shape(1, H, H), shape(1, H, H)),
        10**8, "vvvvhhhv",
        "vv",
        [
            pltpu.VMEM((5, H, H), F32),
            pltpu.VMEM((1, H, H), F32),
            pltpu.VMEM((1, H), F32),
            pltpu.SemaphoreType.DMA((3,)),
        ],
    )(
        group,
        links2,
        links1,
        nodes,
        steps,
        cotangent,
        initial_state,
        recurrent_weight,
    )
    return new_state, adjoint


def solution(mesh):
    return jax.shard_map(
        per_device,
        mesh=mesh,
        in_specs=(
            P("dp", "seq", None),
            P("dp", "seq", None),
            P("dp", None),
            P("dp", "seq", None),
            P(),
            P(),
            P(),
        ),
        out_specs=(P("dp", "seq", None), P("dp", "seq", None)),
        check_vma=False,
    )
```

```python
import jax
import jax.numpy as jnp
from jax import lax
from jax.experimental import pallas as pl
from jax.experimental.pallas import tpu as pltpu
from jax.sharding import PartitionSpec as P

F32 = jnp.float32
BF16 = jnp.bfloat16
H = 128
BLOCKS = 16
ROW_B = 128
ROW_C = 129
ROW_PROJ = 130
ROW_REC = 133
ROW_LAST = 136
ROWS = 144
VMEM_LIMIT = 24 * 1024 * 1024


def split(x):
    hi = x.astype(BF16)
    return hi, (x - hi.astype(F32)).astype(BF16)


def left(x):
    return jnp.concatenate(split(x), axis=1)


def right(x):
    row = jnp.concatenate(split(x), axis=1)
    return jnp.concatenate([row, row], axis=0)


def both_halves(out):
    half = out.shape[1] // 2
    return out[:, :half] + out[:, half:]


def mm(a, b):
    return both_halves(jnp.dot(left(a), right(b), preferred_element_type=F32))


def pad8(row):
    return jnp.broadcast_to(row, (8, H))


def halves(x):
    return jnp.concatenate(split(x), axis=1)


def stacked(x):
    return jnp.concatenate(split(x), axis=0)


def few_rows(x, weights):
    out = jnp.dot(stacked(x), weights, preferred_element_type=F32)
    return both_halves(out[: x.shape[0]] + out[x.shape[0] :])


def vec_mm(row, b):
    return few_rows(pad8(row), halves(b))[:1]


def vec_mm_t(row, b):
    out = lax.dot_general(
        stacked(pad8(row)), stacked(b), (((1,), (1,)), ((), ())), preferred_element_type=F32
    )
    return both_halves(out[:8] + out[8:])[:1]


def eye():
    rows = lax.broadcasted_iota(jnp.int32, (H, H), 0)
    cols = lax.broadcasted_iota(jnp.int32, (H, H), 1)
    return (rows == cols).astype(F32)


def gates(proj, rec, prev):
    reset = jax.nn.sigmoid(proj[0] + rec[0])
    write = jax.nn.sigmoid(proj[1] + rec[1])
    cand = jnp.tanh(proj[2] + reset * rec[2])
    slope = write * (1.0 - cand * cand)
    terms = (
        slope * rec[2] * reset * (1.0 - reset),
        (cand - prev) * write * (1.0 - write),
        slope * reset,
    )
    off = write * cand - (terms[0] * rec[0] + terms[1] * rec[1] + terms[2] * rec[2])
    return write, terms, off


def parts3(x):
    return x[:, :H], x[:, H : 2 * H], x[:, 2 * H :]


def leaf(u, write, terms, ident):
    return u[0] * terms[0] + u[1] * terms[1] + u[2] * terms[2] - ident * write


def compose(early, late):
    lb, lv, lc = early
    rb, rv, rc = late
    prod = mm(jnp.concatenate([lb, pad8(lv)], axis=0), rb)
    return (
        lb + rb + prod[:H],
        lv + rv + prod[H : H + 1],
        lc + rc + vec_mm_t(rc, lb),
    )


def local_kernel(
    x_hbm,
    traj_hbm,
    cot_hbm,
    init_hbm,
    win_hbm,
    wrec_hbm,
    bias_hbm,
    pack_ref,
    nodes_ref,
    steps_hbm,
    x_ref,
    traj_ref,
    cot_ref,
    init_ref,
    win_ref,
    wrec_ref,
    bias_ref,
    steps_ref,
    pairs_ref,
    quads_ref,
    sems,
):
    copies = [
        pltpu.make_async_copy(src, dst, sems.at[i])
        for i, (src, dst) in enumerate(
            (
                (traj_hbm, traj_ref),
                (wrec_hbm, wrec_ref),
                (init_hbm, init_ref),
                (x_hbm, x_ref),
                (win_hbm, win_ref),
                (bias_hbm, bias_ref),
                (cot_hbm, cot_ref),
            )
        )
    ]
    for copy in copies:
        copy.start()
    for copy in copies[:3]:
        copy.wait()
    traj = traj_ref[0]
    rec_in = jnp.concatenate([traj, pad8(init_ref[...])], axis=0)
    rec_all = jnp.dot(
        rec_in, wrec_ref[...], precision=lax.Precision.HIGHEST, preferred_element_type=F32
    )
    rec_init = rec_all[H : H + 1]
    rec_rows = rec_all[:H]
    for copy in copies[3:]:
        copy.wait()
    proj = (
        jnp.dot(x_ref[0], win_ref[...], precision=lax.Precision.HIGHEST, preferred_element_type=F32)
        + bias_ref[...].reshape(1, 3 * H)
    )
    rec = pltpu.roll(rec_rows, 1, 0)
    prev = pltpu.roll(traj, 1, 0)
    write, terms, off = gates(parts3(proj), parts3(rec), prev)
    inner = lax.broadcasted_iota(jnp.int32, (H, H), 0) > 0
    write = jnp.where(inner, write, 0.0)
    terms = [jnp.where(inner, t, 0.0) for t in terms]
    off = jnp.where(inner, off, 0.0)
    for p, rows in enumerate((*terms, write, off)):
        steps_ref[p] = rows
    save = pltpu.make_async_copy(steps_ref, steps_hbm, sems.at[7])
    save.start()

    ident = eye()
    per_block = H // BLOCKS
    u_side, u_back = weights_of(wrec_ref)

    def some_pairs(k, carry):
        fwd, bwd = carry
        base = pl.multiple_of(k * 16, 16)
        for half in range(2):
            rows = [steps_ref[p, pl.ds(base + 8 * half, 8), :] for p in range(4)]
            u = [wrec_ref[:, p * H : (p + 1) * H] for p in range(3)]
            for i in range(4):
                maps = []
                for l in (2 * i, 2 * i + 1):
                    row = [r[l : l + 1] for r in rows]
                    maps.append(leaf(u, row[3], row[:3], ident))
                pairs_ref[8 * k + 4 * half + i] = maps[0] + maps[1] + mm(*maps)
        fwd = forward_step(fwd, steps_ref, k, u_side, per_block)
        _, bwd = backward_step(bwd, steps_ref, cot_ref, per_block - 1 - k, u_back, per_block)
        return fwd, bwd

    zero = jnp.zeros((BLOCKS, H), F32)
    fwd, bwd = lax.fori_loop(0, 8, some_pairs, (zero, zero), unroll=8)
    for k in range(BLOCKS):
        nodes_ref[BLOCKS + k, H:] = two_rows(fwd[k : k + 1], bwd[k : k + 1])

    def joined(ref, i):
        early, late = ref[2 * i], ref[2 * i + 1]
        return early + late + mm(early, late)

    def some_quads(k, carry):
        for i in range(8):
            quads_ref[8 * k + i] = joined(pairs_ref, 8 * k + i)
        return carry

    lax.fori_loop(0, 4, some_quads, 0, unroll=4)

    def some_blocks(k, carry):
        for i in range(8):
            nodes_ref[BLOCKS + 8 * k + i, :H] = joined(quads_ref, 8 * k + i)
        return carry

    lax.fori_loop(0, 2, some_blocks, 0, unroll=2)

    def node(n):
        return nodes_ref[n, :H], nodes_ref[n, H : H + 1], nodes_ref[n, H + 1 : H + 2]

    for n in range(BLOCKS - 1, 0, -1):
        m, v, c = compose(node(2 * n), node(2 * n + 1))
        nodes_ref[n, :H] = m
        nodes_ref[n, H:] = two_rows(v, c)
    nodes_ref[0, :8] = jnp.concatenate([*parts3(rec_init), jnp.zeros((5, H), F32)], axis=0)
    nodes_ref[0, 8:] = jnp.zeros((H, H), F32)
    m, v, c = node(1)
    rec_last = rec_rows[H - 1 : H]
    write_pack(
        pack_ref,
        m,
        [v, c]
        + [proj[0:1, p * H : (p + 1) * H] for p in range(3)]
        + [rec_last[:, p * H : (p + 1) * H] for p in range(3)]
        + [traj[H - 1 : H]],
    )
    save.wait()


def two_rows(v, c):
    return jnp.concatenate([v, c, jnp.zeros((6, H), F32)], axis=0)


def write_pack(pack_ref, m, rows):
    tail = jnp.concatenate(rows + [jnp.zeros((ROWS - H - len(rows), H), F32)], axis=0)
    for i in range(pack_ref.shape[0]):
        pack_ref[i, :H] = m
        pack_ref[i, H:] = tail


def weights_of(wrec_ref):
    u = wrec_ref[...]
    return halves(u), halves(u.T)


def every(ref, l, per_block):
    return ref[pl.ds(l, BLOCKS, stride=per_block), :]


def forward_step(h, steps_ref, l, u_side, per_block):
    term = [every(steps_ref.at[p], l, per_block) for p in range(5)]
    mapped = parts3(few_rows(h, u_side))
    moved = term[0] * mapped[0] + term[1] * mapped[1] + term[2] * mapped[2]
    return h + (moved - term[3] * h) + term[4]


def backward_step(carried, steps_ref, cot_ref, l, u_back, per_block):
    term = [every(steps_ref.at[p], l, per_block) for p in range(4)]
    costate = carried + every(cot_ref.at[0], l, per_block)
    scaled = jnp.concatenate([term[p] * costate for p in range(3)], axis=1)
    back = few_rows(scaled, u_back)
    return costate, costate + (back - term[3] * costate)


def boundaries(group_ref, wrec_ref, ident):
    u = [wrec_ref[:, p * H : (p + 1) * H] for p in range(3)]
    found = []
    for j in range(1, 4):
        proj = [group_ref[j, ROW_PROJ + p : ROW_PROJ + p + 1] for p in range(3)]
        rec = [group_ref[j - 1, ROW_REC + p : ROW_REC + p + 1] for p in range(3)]
        write, terms, off = gates(proj, rec, group_ref[j - 1, ROW_LAST : ROW_LAST + 1])
        found.append((leaf(u, write, terms, ident), off))
    return found


def links(group_ref, wrec_ref):
    ident = eye()
    firsts = boundaries(group_ref, wrec_ref, ident)
    ahead, behind = [], []
    for j in range(3):
        first, off = firsts[j]
        part = group_ref[j, :H]
        prod = mm(group_ref[j, : H + 8], first)
        ahead.append(
            (
                part + first + prod[:H],
                group_ref[j, ROW_B : ROW_B + 1] + off + prod[ROW_B : ROW_B + 1],
            )
        )
        part = group_ref[j + 1, :H]
        cc = group_ref[j + 1, ROW_C : ROW_C + 1]
        prod = mm(jnp.concatenate([first, pad8(off)], axis=0), part)
        behind.append(
            (
                part + first + prod[:H],
                off + prod[H : H + 1] + group_ref[j + 1, ROW_B : ROW_B + 1],
                cc + vec_mm_t(cc, first),
            )
        )
    return ahead, behind


def merge_kernel(group_ref, wrec_ref, pack_ref, links_ref):
    ahead, behind = links(group_ref, wrec_ref)
    for j in range(3):
        m, v = ahead[j]
        links_ref[j, :H] = m
        links_ref[j, H:] = pad8(v)
        m, v, c = behind[j]
        links_ref[3 + j, :H] = m
        links_ref[3 + j, H:] = pad8(c)
    start = (
        group_ref[0, :H],
        group_ref[0, ROW_B : ROW_B + 1],
        group_ref[0, ROW_C : ROW_C + 1],
    )
    m, v, c = compose(compose(start, behind[0]), compose(behind[1], behind[2]))
    write_pack(
        pack_ref,
        m,
        [v, c]
        + [group_ref[0, ROW_PROJ + p : ROW_PROJ + p + 1] for p in range(3)]
        + [group_ref[3, ROW_REC + p : ROW_REC + p + 1] for p in range(3)]
        + [group_ref[3, ROW_LAST : ROW_LAST + 1]],
    )


def places():
    place = lax.axis_index("seq")
    return place // 16, place // 4 % 4, place % 4


def forward_join(early, late):
    prod = mm(jnp.concatenate([early[0], pad8(early[1])], axis=0), late[0])
    return early[0] + late[0] + prod[:H], early[1] + late[1] + prod[H : H + 1]


def adjoint_join(early, late):
    return (
        early[0] + late[0] + mm(early[0], late[0]),
        early[1] + late[1] + vec_mm_t(late[1], early[0]),
    )


def paths_to(own, links_ref):
    ahead = [(links_ref[j, :H], links_ref[j, H : H + 1]) for j in range(3)]
    behind = [(links_ref[3 + j, :H], links_ref[3 + j, H : H + 1]) for j in range(3)]
    keep = lambda on, new, old: tuple(jnp.where(on, n, o) for n, o in zip(new, old))
    none = (jnp.zeros((H, H), F32), jnp.zeros((1, H), F32))
    to = keep(own > 0, ahead[0], none)
    back = keep(own < 3, behind[2], none)
    for j in (1, 2):
        to = keep(own > j, forward_join(to, ahead[j]), to)
        back = keep(own < 3 - j, adjoint_join(behind[2 - j], back), back)
    return to, back


def reach_kernel(
    nodes_ref,
    links1_ref,
    links2_ref,
    wrec_ref,
    maps_hbm,
    vecs_hbm,
    u_hbm,
    ut_hbm,
    maps_ref,
    vecs_ref,
    u_ref,
    ut_ref,
    sems,
):
    _, middle, near = places()
    to1, back1 = paths_to(near, links1_ref)
    to2, back2 = paths_to(middle, links2_ref)
    none = (jnp.zeros((H, H), F32), jnp.zeros((1, H), F32))

    def put(slot, found, flip):
        m, v = found or none
        maps_ref[slot] = halves(m.T if flip else m)
        vecs_ref[slot : slot + 1] = v

    put(2 * BLOCKS, forward_join(to2, to1), False)
    put(2 * BLOCKS + 1, adjoint_join(back1, back2), True)
    vecs_ref[2 * BLOCKS + 2 :] = jnp.zeros((6, H), F32)

    def node(n, row):
        return nodes_ref[n, :H], nodes_ref[n, H + row : H + row + 1]

    before, after = {1: None}, {1: None}
    for n in range(1, BLOCKS):
        before[2 * n] = before[n]
        first = node(2 * n, 0)
        before[2 * n + 1] = first if before[n] is None else forward_join(before[n], first)
        after[2 * n + 1] = after[n]
        last = node(2 * n + 1, 1)
        after[2 * n] = last if after[n] is None else adjoint_join(last, after[n])
    for k in range(BLOCKS):
        put(k, before[BLOCKS + k], False)
        put(BLOCKS + k, after[BLOCKS + k], True)
    u = wrec_ref[...]
    u_ref[...] = halves(u)
    ut_ref[...] = halves(u.T)
    copies = [
        pltpu.make_async_copy(src, dst, sems.at[i])
        for i, (src, dst) in enumerate(
            ((maps_ref, maps_hbm), (vecs_ref, vecs_hbm), (u_ref, u_hbm), (ut_ref, ut_hbm))
        )
    ]
    for copy in copies:
        copy.start()
    for copy in copies:
        copy.wait()


def moved_by(vector, weights):
    return few_rows(pad8(vector), weights)[:1]


def apply_kernel(
    group_ref,
    nodes_ref,
    wrec_ref,
    maps_hbm,
    vecs_hbm,
    u_hbm,
    ut_hbm,
    steps_hbm,
    cot_hbm,
    init_hbm,
    state_ref,
    adjoint_ref,
    maps_ref,
    vecs_ref,
    u_ref,
    ut_ref,
    steps_ref,
    cot_ref,
    init_ref,
    sems,
):
    copies = [
        pltpu.make_async_copy(src, dst, sems.at[i])
        for i, (src, dst) in enumerate(
            (
                (init_hbm, init_ref),
                (maps_hbm, maps_ref),
                (vecs_hbm, vecs_ref),
                (u_hbm, u_ref),
                (ut_hbm, ut_ref),
                (steps_hbm, steps_ref),
                (cot_hbm, cot_ref),
            )
        )
    ]
    for copy in copies:
        copy.start()
    per_block = H // BLOCKS
    ahead, behind = links(group_ref, wrec_ref)
    copies[0].wait()
    init = init_ref[...]
    rec = [nodes_ref[0, p : p + 1] for p in range(3)]
    write, terms, off = gates(
        [group_ref[0, ROW_PROJ + p : ROW_PROJ + p + 1] for p in range(3)], rec, init
    )
    state = (
        init
        + (terms[0] * rec[0] + terms[1] * rec[1] + terms[2] * rec[2])
        - write * init
        + off
    )
    costate = jnp.zeros((1, H), F32)
    own = places()[0]
    for j in range(3):
        moved = state + vec_mm(state, ahead[j][0]) + ahead[j][1]
        state = jnp.where(j < own, moved, state)
        i = 2 - j
        moved = costate + vec_mm_t(costate, behind[i][0]) + behind[i][2]
        costate = jnp.where(i >= own, moved, costate)
    for copy in copies[1:]:
        copy.wait()
    at = 2 * BLOCKS
    state = state + moved_by(state, maps_ref[at]) + vecs_ref[at : at + 1]
    costate = costate + moved_by(costate, maps_ref[at + 1]) + vecs_ref[at + 1 : at + 2]
    fwd = jnp.concatenate([moved_by(state, maps_ref[k]) for k in range(BLOCKS)], axis=0)
    fwd = state + fwd + vecs_ref[:BLOCKS]
    bwd = jnp.concatenate([moved_by(costate, maps_ref[BLOCKS + k]) for k in range(BLOCKS)], axis=0)
    bwd = costate + bwd + vecs_ref[BLOCKS : 2 * BLOCKS]
    u_side, u_back = u_ref[...], ut_ref[...]
    for l in range(per_block):
        fwd = forward_step(fwd, steps_ref, l, u_side, per_block)
        state_ref.at[0][pl.ds(l, BLOCKS, stride=per_block), :] = fwd
        back = per_block - 1 - l
        out, bwd = backward_step(bwd, steps_ref, cot_ref, back, u_back, per_block)
        adjoint_ref.at[0][pl.ds(back, BLOCKS, stride=per_block), :] = out


def call(kernel, out_shape, flops, spaces, outs, scratch=()):
    kinds = {"s": pltpu.SMEM, "v": pltpu.VMEM, "h": pltpu.HBM}
    run = pl.pallas_call(
        kernel,
        out_shape=tuple(
            pltpu.HBM(o.shape, o.dtype) if k == "h" else o for k, o in zip(outs, out_shape)
        ),
        in_specs=[pl.BlockSpec(memory_space=kinds[k]) for k in spaces],
        out_specs=tuple(pl.BlockSpec(memory_space=kinds[k]) for k in outs),
        scratch_shapes=list(scratch),
        compiler_params=pltpu.CompilerParams(vmem_limit_bytes=VMEM_LIMIT),
        cost_estimate=pl.CostEstimate(flops=flops, bytes_accessed=2**20, transcendentals=0),
    )

    def placed(*args):
        return run(
            *(
                pltpu.with_memory_space_constraint(a, pltpu.HBM) if k == "h" else a
                for k, a in zip(spaces, args)
            )
        )

    return placed


def group_lists(count):
    near = [list(range(s, s + 4)) for s in range(0, count, 4)]
    middle = [
        [16 * y + i, 16 * y + 4 + i, 16 * y + 11 - i, 16 * y + 15 - i]
        for y in range(count // 16)
        for i in range(4)
    ]
    far = [[16 * y + z for y in range(4)] for z in range(16)]
    return near, middle, far


def shape(*dims):
    return jax.ShapeDtypeStruct(dims, F32)


def per_device(
    inputs, trajectory, initial_state, cotangent, in_weight, recurrent_weight, gate_bias
):
    near, middle, far = group_lists(lax.axis_size("seq"))
    pack, nodes, steps = call(
        local_kernel,
        (
            shape(4, ROWS, H),
            shape(2 * BLOCKS, H + 8, H),
            shape(5, H, H),
        ),
        2 * 10**9,
        "hhhhhhh",
        "vvh",
        [
            pltpu.VMEM((1, H, H), F32),
            pltpu.VMEM((1, H, H), F32),
            pltpu.VMEM((1, H, H), F32),
            pltpu.VMEM((1, H), F32),
            pltpu.VMEM((H, 3 * H), F32),
            pltpu.VMEM((H, 3 * H), F32),
            pltpu.VMEM((3 * H,), F32),
            pltpu.VMEM((5, H, H), F32),
            pltpu.VMEM((64, H, H), F32),
            pltpu.VMEM((32, H, H), F32),
            pltpu.SemaphoreType.DMA((8,)),
        ],
    )(
        inputs,
        trajectory,
        cotangent,
        initial_state,
        in_weight,
        recurrent_weight,
        gate_bias,
    )
    merge = call(
        merge_kernel, (shape(4, ROWS, H), shape(6, H + 8, H)), 10**8, "vv", "vv"
    )

    def exchange(packed, groups):
        return lax.all_to_all(packed, "seq", 0, 0, axis_index_groups=groups)

    pack, links1 = merge(exchange(pack, near), recurrent_weight)
    pack, links2 = merge(exchange(pack, middle), recurrent_weight)
    group = exchange(pack, far)
    found = (
        (2 * BLOCKS + 2, H, 2 * H),
        (2 * BLOCKS + 8, H),
        (H, 6 * H),
        (3 * H, 2 * H),
    )
    kinds = (BF16, F32, BF16, BF16)
    buffers = [pltpu.VMEM(dims, kind) for dims, kind in zip(found, kinds)]
    reached = call(
        reach_kernel,
        tuple(jax.ShapeDtypeStruct(dims, kind) for dims, kind in zip(found, kinds)),
        5 * 10**8,
        "vvvv",
        "hhhh",
        buffers + [pltpu.SemaphoreType.DMA((4,))],
    )(nodes, links1, links2, recurrent_weight)
    new_state, adjoint = call(
        apply_kernel,
        (shape(1, H, H), shape(1, H, H)),
        10**8,
        "vvvhhhhhhh",
        "vv",
        buffers
        + [
            pltpu.VMEM((5, H, H), F32),
            pltpu.VMEM((1, H, H), F32),
            pltpu.VMEM((1, H), F32),
            pltpu.SemaphoreType.DMA((7,)),
        ],
    )(group, nodes, recurrent_weight, *reached, steps, cotangent, initial_state)
    return new_state, adjoint


def solution(mesh):
    return jax.shard_map(
        per_device,
        mesh=mesh,
        in_specs=(
            P("dp", "seq", None),
            P("dp", "seq", None),
            P("dp", None),
            P("dp", "seq", None),
            P(),
            P(),
            P(),
        ),
        out_specs=(P("dp", "seq", None), P("dp", "seq", None)),
        check_vma=False,
    )
```

```python
import functools

import jax
import jax.numpy as jnp
from jax import lax
from jax.experimental import pallas as pl
from jax.experimental.pallas import tpu as pltpu
from jax.sharding import PartitionSpec as P

F32 = jnp.float32
BF16 = jnp.bfloat16
H = 128
BLOCKS = 16
ROW_B = 128
ROW_C = 129
ROW_PROJ = 130
ROW_REC = 133
ROW_LAST = 136
ROWS = 144
VMEM_LIMIT = 24 * 1024 * 1024


def split(x):
    hi = x.astype(BF16)
    return hi, (x - hi.astype(F32)).astype(BF16)


def left(x):
    return jnp.concatenate(split(x), axis=1)


def right(x):
    row = jnp.concatenate(split(x), axis=1)
    return jnp.concatenate([row, row], axis=0)


def both_halves(out):
    half = out.shape[1] // 2
    return out[:, :half] + out[:, half:]


def mm(a, b):
    return both_halves(jnp.dot(left(a), right(b), preferred_element_type=F32))


def pad8(row):
    return jnp.broadcast_to(row, (8, H))


def halves(x):
    return jnp.concatenate(split(x), axis=1)


def stacked(x):
    return jnp.concatenate(split(x), axis=0)


def few_rows(x, weights):
    out = jnp.dot(stacked(x), weights, preferred_element_type=F32)
    return both_halves(out[: x.shape[0]] + out[x.shape[0] :])


def vec_mm(row, b):
    return few_rows(pad8(row), halves(b))[:1]


def vec_mm_t(row, b):
    out = lax.dot_general(
        stacked(pad8(row)), stacked(b), (((1,), (1,)), ((), ())), preferred_element_type=F32
    )
    return both_halves(out[:8] + out[8:])[:1]


def eye():
    rows = lax.broadcasted_iota(jnp.int32, (H, H), 0)
    cols = lax.broadcasted_iota(jnp.int32, (H, H), 1)
    return (rows == cols).astype(F32)


def gates(proj, rec, prev):
    reset = jax.nn.sigmoid(proj[0] + rec[0])
    write = jax.nn.sigmoid(proj[1] + rec[1])
    cand = jnp.tanh(proj[2] + reset * rec[2])
    slope = write * (1.0 - cand * cand)
    terms = (
        slope * rec[2] * reset * (1.0 - reset),
        (cand - prev) * write * (1.0 - write),
        slope * reset,
    )
    off = write * cand - (terms[0] * rec[0] + terms[1] * rec[1] + terms[2] * rec[2])
    return write, terms, off


def parts3(x):
    return x[:, :H], x[:, H : 2 * H], x[:, 2 * H :]


def leaf(u, write, terms, ident):
    return u[0] * terms[0] + u[1] * terms[1] + u[2] * terms[2] - ident * write


def compose(early, late):
    lb, lv, lc = early
    rb, rv, rc = late
    prod = mm(jnp.concatenate([lb, pad8(lv)], axis=0), rb)
    return (
        lb + rb + prod[:H],
        lv + rv + prod[H : H + 1],
        lc + rc + vec_mm_t(rc, lb),
    )


def local_kernel(
    x_hbm,
    traj_hbm,
    cot_hbm,
    init_hbm,
    win_hbm,
    wrec_hbm,
    bias_hbm,
    pack_ref,
    nodes_ref,
    steps_hbm,
    x_ref,
    traj_ref,
    cot_ref,
    init_ref,
    win_ref,
    wrec_ref,
    bias_ref,
    steps_ref,
    pairs_ref,
    quads_ref,
    sems,
):
    copies = [
        pltpu.make_async_copy(src, dst, sems.at[i])
        for i, (src, dst) in enumerate(
            (
                (traj_hbm, traj_ref),
                (wrec_hbm, wrec_ref),
                (init_hbm, init_ref),
                (x_hbm, x_ref),
                (win_hbm, win_ref),
                (bias_hbm, bias_ref),
                (cot_hbm, cot_ref),
            )
        )
    ]
    for copy in copies:
        copy.start()
    for copy in copies[:3]:
        copy.wait()
    traj = traj_ref[0]
    rec_in = jnp.concatenate([traj, pad8(init_ref[...])], axis=0)
    rec_all = jnp.dot(
        rec_in, wrec_ref[...], precision=lax.Precision.HIGHEST, preferred_element_type=F32
    )
    rec_init = rec_all[H : H + 1]
    rec_rows = rec_all[:H]
    for copy in copies[3:]:
        copy.wait()
    proj = (
        jnp.dot(x_ref[0], win_ref[...], precision=lax.Precision.HIGHEST, preferred_element_type=F32)
        + bias_ref[...].reshape(1, 3 * H)
    )
    rec = pltpu.roll(rec_rows, 1, 0)
    prev = pltpu.roll(traj, 1, 0)
    write, terms, off = gates(parts3(proj), parts3(rec), prev)
    inner = lax.broadcasted_iota(jnp.int32, (H, H), 0) > 0
    write = jnp.where(inner, write, 0.0)
    terms = [jnp.where(inner, t, 0.0) for t in terms]
    off = jnp.where(inner, off, 0.0)
    for p, rows in enumerate((*terms, write, off)):
        steps_ref[p] = rows
    save = pltpu.make_async_copy(steps_ref, steps_hbm, sems.at[7])
    save.start()

    ident = eye()
    per_block = H // BLOCKS
    u_side, u_back = weights_of(wrec_ref)

    def some_pairs(k, carry):
        fwd, bwd = carry
        base = pl.multiple_of(k * 16, 16)
        for half in range(2):
            rows = [steps_ref[p, pl.ds(base + 8 * half, 8), :] for p in range(4)]
            u = [wrec_ref[:, p * H : (p + 1) * H] for p in range(3)]
            for i in range(4):
                maps = []
                for l in (2 * i, 2 * i + 1):
                    row = [r[l : l + 1] for r in rows]
                    maps.append(leaf(u, row[3], row[:3], ident))
                pairs_ref[8 * k + 4 * half + i] = maps[0] + maps[1] + mm(*maps)
        fwd = forward_step(fwd, steps_ref, k, u_side, per_block)
        _, bwd = backward_step(bwd, steps_ref, cot_ref, per_block - 1 - k, u_back, per_block)
        return fwd, bwd

    zero = jnp.zeros((BLOCKS, H), F32)
    fwd, bwd = lax.fori_loop(0, 8, some_pairs, (zero, zero), unroll=8)
    for k in range(BLOCKS):
        nodes_ref[BLOCKS + k, H:] = two_rows(fwd[k : k + 1], bwd[k : k + 1])

    def joined(ref, i):
        early, late = ref[2 * i], ref[2 * i + 1]
        return early + late + mm(early, late)

    def some_quads(k, carry):
        for i in range(8):
            quads_ref[8 * k + i] = joined(pairs_ref, 8 * k + i)
        return carry

    lax.fori_loop(0, 4, some_quads, 0, unroll=4)

    def some_blocks(k, carry):
        for i in range(8):
            nodes_ref[BLOCKS + 8 * k + i, :H] = joined(quads_ref, 8 * k + i)
        return carry

    lax.fori_loop(0, 2, some_blocks, 0, unroll=2)

    def node(n):
        return nodes_ref[n, :H], nodes_ref[n, H : H + 1], nodes_ref[n, H + 1 : H + 2]

    for n in range(BLOCKS - 1, 0, -1):
        m, v, c = compose(node(2 * n), node(2 * n + 1))
        nodes_ref[n, :H] = m
        nodes_ref[n, H:] = two_rows(v, c)
    nodes_ref[0, :8] = jnp.concatenate([*parts3(rec_init), jnp.zeros((5, H), F32)], axis=0)
    nodes_ref[0, 8:] = jnp.zeros((H, H), F32)
    m, v, c = node(1)
    rec_last = rec_rows[H - 1 : H]
    write_pack(
        pack_ref,
        m,
        [v, c]
        + [proj[0:1, p * H : (p + 1) * H] for p in range(3)]
        + [rec_last[:, p * H : (p + 1) * H] for p in range(3)]
        + [traj[H - 1 : H]],
    )
    save.wait()


def two_rows(v, c):
    return jnp.concatenate([v, c, jnp.zeros((6, H), F32)], axis=0)


def write_pack(pack_ref, m, rows):
    tail = jnp.concatenate(rows + [jnp.zeros((ROWS - H - len(rows), H), F32)], axis=0)
    for i in range(pack_ref.shape[0]):
        pack_ref[i, :H] = m
        pack_ref[i, H:] = tail


def weights_of(wrec_ref):
    u = wrec_ref[...]
    return halves(u), halves(u.T)


def every(ref, l, per_block):
    return ref[pl.ds(l, BLOCKS, stride=per_block), :]


def forward_step(h, steps_ref, l, u_side, per_block):
    term = [every(steps_ref.at[p], l, per_block) for p in range(5)]
    mapped = parts3(few_rows(h, u_side))
    moved = term[0] * mapped[0] + term[1] * mapped[1] + term[2] * mapped[2]
    return h + (moved - term[3] * h) + term[4]


def backward_step(carried, steps_ref, cot_ref, l, u_back, per_block):
    term = [every(steps_ref.at[p], l, per_block) for p in range(4)]
    costate = carried + every(cot_ref.at[0], l, per_block)
    scaled = jnp.concatenate([term[p] * costate for p in range(3)], axis=1)
    back = few_rows(scaled, u_back)
    return costate, costate + (back - term[3] * costate)


def boundaries(group_ref, wrec_ref, ident):
    u = [wrec_ref[:, p * H : (p + 1) * H] for p in range(3)]
    found = []
    for j in range(1, 4):
        proj = [group_ref[j, ROW_PROJ + p : ROW_PROJ + p + 1] for p in range(3)]
        rec = [group_ref[j - 1, ROW_REC + p : ROW_REC + p + 1] for p in range(3)]
        write, terms, off = gates(proj, rec, group_ref[j - 1, ROW_LAST : ROW_LAST + 1])
        found.append((leaf(u, write, terms, ident), off))
    return found


def links(group_ref, wrec_ref):
    ident = eye()
    firsts = boundaries(group_ref, wrec_ref, ident)
    ahead, behind = [], []
    for j in range(3):
        first, off = firsts[j]
        part = group_ref[j, :H]
        prod = mm(group_ref[j, : H + 8], first)
        ahead.append(
            (
                part + first + prod[:H],
                group_ref[j, ROW_B : ROW_B + 1] + off + prod[ROW_B : ROW_B + 1],
            )
        )
        part = group_ref[j + 1, :H]
        cc = group_ref[j + 1, ROW_C : ROW_C + 1]
        prod = mm(jnp.concatenate([first, pad8(off)], axis=0), part)
        behind.append(
            (
                part + first + prod[:H],
                off + prod[H : H + 1] + group_ref[j + 1, ROW_B : ROW_B + 1],
                cc + vec_mm_t(cc, first),
            )
        )
    return ahead, behind


def merge_kernel(group_ref, wrec_ref, pack_ref, links_ref):
    ahead, behind = links(group_ref, wrec_ref)
    for j in range(3):
        m, v = ahead[j]
        links_ref[j, :H] = m
        links_ref[j, H:] = pad8(v)
        m, v, c = behind[j]
        links_ref[3 + j, :H] = m
        links_ref[3 + j, H:] = pad8(c)
    start = (
        group_ref[0, :H],
        group_ref[0, ROW_B : ROW_B + 1],
        group_ref[0, ROW_C : ROW_C + 1],
    )
    m, v, c = compose(compose(start, behind[0]), compose(behind[1], behind[2]))
    write_pack(
        pack_ref,
        m,
        [v, c]
        + [group_ref[0, ROW_PROJ + p : ROW_PROJ + p + 1] for p in range(3)]
        + [group_ref[3, ROW_REC + p : ROW_REC + p + 1] for p in range(3)]
        + [group_ref[3, ROW_LAST : ROW_LAST + 1]],
    )


def places():
    place = lax.axis_index("seq")
    return place // 16, place % 4


def forward_join(early, late):
    prod = mm(jnp.concatenate([early[0], pad8(early[1])], axis=0), late[0])
    return early[0] + late[0] + prod[:H], early[1] + late[1] + prod[H : H + 1]


def adjoint_join(early, late):
    return (
        early[0] + late[0] + mm(early[0], late[0]),
        early[1] + late[1] + vec_mm_t(late[1], early[0]),
    )


def paths_to(own, links_ref):
    ahead = [(links_ref[j, :H], links_ref[j, H : H + 1]) for j in range(3)]
    behind = [(links_ref[3 + j, :H], links_ref[3 + j, H : H + 1]) for j in range(3)]
    keep = lambda on, new, old: tuple(jnp.where(on, n, o) for n, o in zip(new, old))
    none = (jnp.zeros((H, H), F32), jnp.zeros((1, H), F32))
    to = keep(own > 0, ahead[0], none)
    back = keep(own < 3, behind[2], none)
    for j in (1, 2):
        to = keep(own > j, forward_join(to, ahead[j]), to)
        back = keep(own < 3 - j, adjoint_join(behind[2 - j], back), back)
    return to, back


def pair_kernel(own_ref, other_ref, wrec_ref, pack_ref, path_ref, *, bit):
    second = lax.axis_index("seq") // bit % 2 == 1
    own, other = own_ref[0], other_ref[0]
    early = jnp.where(second, other, own)
    late = jnp.where(second, own, other)
    u = [wrec_ref[:, p * H : (p + 1) * H] for p in range(3)]
    write, terms, off = gates(
        [late[ROW_PROJ + p : ROW_PROJ + p + 1] for p in range(3)],
        [early[ROW_REC + p : ROW_REC + p + 1] for p in range(3)],
        early[ROW_LAST : ROW_LAST + 1],
    )
    first = leaf(u, write, terms, eye())
    early_v, early_c = early[ROW_B : ROW_B + 1], early[ROW_C : ROW_C + 1]
    late_v, late_c = late[ROW_B : ROW_B + 1], late[ROW_C : ROW_C + 1]
    ahead = forward_join((early[:H], early_v), (first, off))
    prod = mm(jnp.concatenate([first, pad8(off)], axis=0), late[:H])
    behind = (
        first + late[:H] + prod[:H],
        off + prod[H : H + 1] + late_v,
        late_c + vec_mm_t(late_c, first),
    )
    path_ref[0, :H] = jnp.where(second, ahead[0], 0.0)
    path_ref[0, H:] = pad8(jnp.where(second, ahead[1], 0.0))
    path_ref[1, :H] = jnp.where(second, 0.0, behind[0])
    path_ref[1, H:] = pad8(jnp.where(second, 0.0, behind[2]))
    m, v, c = compose((early[:H], early_v, early_c), behind)
    write_pack(
        pack_ref,
        m,
        [v, c]
        + [early[ROW_PROJ + p : ROW_PROJ + p + 1] for p in range(3)]
        + [late[ROW_REC + p : ROW_REC + p + 1] for p in range(3)]
        + [late[ROW_LAST : ROW_LAST + 1]],
    )


def reach_kernel(
    nodes_ref,
    links1_ref,
    path2_ref,
    path3_ref,
    wrec_ref,
    maps_hbm,
    vecs_hbm,
    u_hbm,
    ut_hbm,
    maps_ref,
    vecs_ref,
    u_ref,
    ut_ref,
    sems,
):
    to, back = paths_to(places()[1], links1_ref)
    for path_ref in (path2_ref, path3_ref):
        to = forward_join((path_ref[0, :H], path_ref[0, H : H + 1]), to)
        back = adjoint_join(back, (path_ref[1, :H], path_ref[1, H : H + 1]))
    none = (jnp.zeros((H, H), F32), jnp.zeros((1, H), F32))

    def put(slot, found, flip):
        m, v = found or none
        maps_ref[slot] = halves(m.T if flip else m)
        vecs_ref[slot : slot + 1] = v

    put(2 * BLOCKS, to, False)
    put(2 * BLOCKS + 1, back, True)
    vecs_ref[2 * BLOCKS + 2 :] = jnp.zeros((6, H), F32)

    def node(n, row):
        return nodes_ref[n, :H], nodes_ref[n, H + row : H + row + 1]

    before, after = {1: None}, {1: None}
    for n in range(1, BLOCKS):
        before[2 * n] = before[n]
        first = node(2 * n, 0)
        before[2 * n + 1] = first if before[n] is None else forward_join(before[n], first)
        after[2 * n + 1] = after[n]
        last = node(2 * n + 1, 1)
        after[2 * n] = last if after[n] is None else adjoint_join(last, after[n])
    for k in range(BLOCKS):
        put(k, before[BLOCKS + k], False)
        put(BLOCKS + k, after[BLOCKS + k], True)
    u = wrec_ref[...]
    u_ref[...] = halves(u)
    ut_ref[...] = halves(u.T)
    copies = [
        pltpu.make_async_copy(src, dst, sems.at[i])
        for i, (src, dst) in enumerate(
            ((maps_ref, maps_hbm), (vecs_ref, vecs_hbm), (u_ref, u_hbm), (ut_ref, ut_hbm))
        )
    ]
    for copy in copies:
        copy.start()
    for copy in copies:
        copy.wait()


def moved_by(vector, weights):
    return few_rows(pad8(vector), weights)[:1]


def apply_kernel(
    group_ref,
    nodes_ref,
    wrec_ref,
    maps_hbm,
    vecs_hbm,
    u_hbm,
    ut_hbm,
    steps_hbm,
    cot_hbm,
    init_hbm,
    state_ref,
    adjoint_ref,
    maps_ref,
    vecs_ref,
    u_ref,
    ut_ref,
    steps_ref,
    cot_ref,
    init_ref,
    sems,
):
    copies = [
        pltpu.make_async_copy(src, dst, sems.at[i])
        for i, (src, dst) in enumerate(
            (
                (init_hbm, init_ref),
                (maps_hbm, maps_ref),
                (vecs_hbm, vecs_ref),
                (u_hbm, u_ref),
                (ut_hbm, ut_ref),
                (steps_hbm, steps_ref),
                (cot_hbm, cot_ref),
            )
        )
    ]
    for copy in copies:
        copy.start()
    per_block = H // BLOCKS
    ahead, behind = links(group_ref, wrec_ref)
    copies[0].wait()
    init = init_ref[...]
    rec = [nodes_ref[0, p : p + 1] for p in range(3)]
    write, terms, off = gates(
        [group_ref[0, ROW_PROJ + p : ROW_PROJ + p + 1] for p in range(3)], rec, init
    )
    state = (
        init
        + (terms[0] * rec[0] + terms[1] * rec[1] + terms[2] * rec[2])
        - write * init
        + off
    )
    costate = jnp.zeros((1, H), F32)
    own = places()[0]
    for j in range(3):
        moved = state + vec_mm(state, ahead[j][0]) + ahead[j][1]
        state = jnp.where(j < own, moved, state)
        i = 2 - j
        moved = costate + vec_mm_t(costate, behind[i][0]) + behind[i][2]
        costate = jnp.where(i >= own, moved, costate)
    for copy in copies[1:]:
        copy.wait()
    at = 2 * BLOCKS
    state = state + moved_by(state, maps_ref[at]) + vecs_ref[at : at + 1]
    costate = costate + moved_by(costate, maps_ref[at + 1]) + vecs_ref[at + 1 : at + 2]
    fwd = jnp.concatenate([moved_by(state, maps_ref[k]) for k in range(BLOCKS)], axis=0)
    fwd = state + fwd + vecs_ref[:BLOCKS]
    bwd = jnp.concatenate([moved_by(costate, maps_ref[BLOCKS + k]) for k in range(BLOCKS)], axis=0)
    bwd = costate + bwd + vecs_ref[BLOCKS : 2 * BLOCKS]
    u_side, u_back = u_ref[...], ut_ref[...]
    for l in range(per_block):
        fwd = forward_step(fwd, steps_ref, l, u_side, per_block)
        state_ref.at[0][pl.ds(l, BLOCKS, stride=per_block), :] = fwd
        back = per_block - 1 - l
        out, bwd = backward_step(bwd, steps_ref, cot_ref, back, u_back, per_block)
        adjoint_ref.at[0][pl.ds(back, BLOCKS, stride=per_block), :] = out


def call(kernel, out_shape, flops, spaces, outs, scratch=()):
    kinds = {"s": pltpu.SMEM, "v": pltpu.VMEM, "h": pltpu.HBM}
    run = pl.pallas_call(
        kernel,
        out_shape=tuple(
            pltpu.HBM(o.shape, o.dtype) if k == "h" else o for k, o in zip(outs, out_shape)
        ),
        in_specs=[pl.BlockSpec(memory_space=kinds[k]) for k in spaces],
        out_specs=tuple(pl.BlockSpec(memory_space=kinds[k]) for k in outs),
        scratch_shapes=list(scratch),
        compiler_params=pltpu.CompilerParams(vmem_limit_bytes=VMEM_LIMIT),
        cost_estimate=pl.CostEstimate(flops=flops, bytes_accessed=2**20, transcendentals=0),
    )

    def placed(*args):
        return run(
            *(
                pltpu.with_memory_space_constraint(a, pltpu.HBM) if k == "h" else a
                for k, a in zip(spaces, args)
            )
        )

    return placed


def group_lists(count):
    near = [list(range(s, s + 4)) for s in range(0, count, 4)]
    far = [[16 * y + z for y in range(4)] for z in range(16)]
    return near, far


def shape(*dims):
    return jax.ShapeDtypeStruct(dims, F32)


def per_device(
    inputs, trajectory, initial_state, cotangent, in_weight, recurrent_weight, gate_bias
):
    count = lax.axis_size("seq")
    near, far = group_lists(count)
    pack, nodes, steps = call(
        local_kernel,
        (
            shape(4, ROWS, H),
            shape(2 * BLOCKS, H + 8, H),
            shape(5, H, H),
        ),
        2 * 10**9,
        "hhhhhhh",
        "vvh",
        [
            pltpu.VMEM((1, H, H), F32),
            pltpu.VMEM((1, H, H), F32),
            pltpu.VMEM((1, H, H), F32),
            pltpu.VMEM((1, H), F32),
            pltpu.VMEM((H, 3 * H), F32),
            pltpu.VMEM((H, 3 * H), F32),
            pltpu.VMEM((3 * H,), F32),
            pltpu.VMEM((5, H, H), F32),
            pltpu.VMEM((64, H, H), F32),
            pltpu.VMEM((32, H, H), F32),
            pltpu.SemaphoreType.DMA((8,)),
        ],
    )(
        inputs,
        trajectory,
        cotangent,
        initial_state,
        in_weight,
        recurrent_weight,
        gate_bias,
    )
    merge = call(
        merge_kernel, (shape(1, ROWS, H), shape(6, H + 8, H)), 10**8, "vv", "vv"
    )

    def exchange(packed, groups):
        return lax.all_to_all(packed, "seq", 0, 0, axis_index_groups=groups)

    def pair(packed, bit, flip, copies):
        other = lax.ppermute(packed, "seq", [(i, i ^ flip) for i in range(count)])
        return call(
            functools.partial(pair_kernel, bit=bit),
            (shape(copies, ROWS, H), shape(2, H + 8, H)),
            10**8,
            "vvv",
            "vv",
        )(packed, other, recurrent_weight)

    pack, links1 = merge(exchange(pack, near), recurrent_weight)
    pack, path2 = pair(pack, 4, 4, 1)
    pack, path3 = pair(pack, 8, 12, 4)
    group = exchange(pack, far)
    found = (
        (2 * BLOCKS + 2, H, 2 * H),
        (2 * BLOCKS + 8, H),
        (H, 6 * H),
        (3 * H, 2 * H),
    )
    kinds = (BF16, F32, BF16, BF16)
    buffers = [pltpu.VMEM(dims, kind) for dims, kind in zip(found, kinds)]
    reached = call(
        reach_kernel,
        tuple(jax.ShapeDtypeStruct(dims, kind) for dims, kind in zip(found, kinds)),
        5 * 10**8,
        "vvvvv",
        "hhhh",
        buffers + [pltpu.SemaphoreType.DMA((4,))],
    )(nodes, links1, path2, path3, recurrent_weight)
    new_state, adjoint = call(
        apply_kernel,
        (shape(1, H, H), shape(1, H, H)),
        10**8,
        "vvvhhhhhhh",
        "vv",
        buffers
        + [
            pltpu.VMEM((5, H, H), F32),
            pltpu.VMEM((1, H, H), F32),
            pltpu.VMEM((1, H), F32),
            pltpu.SemaphoreType.DMA((7,)),
        ],
    )(group, nodes, recurrent_weight, *reached, steps, cotangent, initial_state)
    return new_state, adjoint


def solution(mesh):
    return jax.shard_map(
        per_device,
        mesh=mesh,
        in_specs=(
            P("dp", "seq", None),
            P("dp", "seq", None),
            P("dp", None),
            P("dp", "seq", None),
            P(),
            P(),
            P(),
        ),
        out_specs=(P("dp", "seq", None), P("dp", "seq", None)),
        check_vma=False,
    )
```

```python
import functools

import jax
import jax.numpy as jnp
from jax import lax
from jax.experimental import pallas as pl
from jax.experimental.pallas import tpu as pltpu
from jax.sharding import PartitionSpec as P

F32 = jnp.float32
BF16 = jnp.bfloat16
H = 128
BLOCKS = 16
ROW_B = 128
ROW_C = 129
ROW_PROJ = 130
ROW_REC = 133
ROW_LAST = 136
ROWS = 144
VMEM_LIMIT = 24 * 1024 * 1024


def split(x):
    hi = x.astype(BF16)
    return hi, (x - hi.astype(F32)).astype(BF16)


def left(x):
    return jnp.concatenate(split(x), axis=1)


def right(x):
    row = jnp.concatenate(split(x), axis=1)
    return jnp.concatenate([row, row], axis=0)


def both_halves(out):
    half = out.shape[1] // 2
    return out[:, :half] + out[:, half:]


def mm(a, b):
    return both_halves(jnp.dot(left(a), right(b), preferred_element_type=F32))


def pad8(row):
    return jnp.broadcast_to(row, (8, H))


def halves(x):
    return jnp.concatenate(split(x), axis=1)


def stacked(x):
    return jnp.concatenate(split(x), axis=0)


def few_rows(x, weights):
    out = jnp.dot(stacked(x), weights, preferred_element_type=F32)
    return both_halves(out[: x.shape[0]] + out[x.shape[0] :])


def vec_mm(row, b):
    return few_rows(pad8(row), halves(b))[:1]


def vec_mm_t(row, b):
    return vec_mm(row, b.T)


def eye():
    rows = lax.broadcasted_iota(jnp.int32, (H, H), 0)
    cols = lax.broadcasted_iota(jnp.int32, (H, H), 1)
    return (rows == cols).astype(F32)


def gates(proj, rec, prev):
    reset = jax.nn.sigmoid(proj[0] + rec[0])
    write = jax.nn.sigmoid(proj[1] + rec[1])
    cand = jnp.tanh(proj[2] + reset * rec[2])
    slope = write * (1.0 - cand * cand)
    terms = (
        slope * rec[2] * reset * (1.0 - reset),
        (cand - prev) * write * (1.0 - write),
        slope * reset,
    )
    off = write * cand - (terms[0] * rec[0] + terms[1] * rec[1] + terms[2] * rec[2])
    return write, terms, off


def parts3(x):
    return x[:, :H], x[:, H : 2 * H], x[:, 2 * H :]


def leaf(u, write, terms, ident):
    return u[0] * terms[0] + u[1] * terms[1] + u[2] * terms[2] - ident * write


def compose(early, late):
    lb, lv, lc = early
    rb, rv, rc = late
    prod = mm(jnp.concatenate([lb, pad8(lv)], axis=0), rb)
    return (
        lb + rb + prod[:H],
        lv + rv + prod[H : H + 1],
        lc + rc + vec_mm_t(rc, lb),
    )


def local_kernel(
    x_hbm,
    traj_hbm,
    cot_hbm,
    init_hbm,
    win_hbm,
    wrec_hbm,
    bias_hbm,
    pack_ref,
    nodes_ref,
    steps_hbm,
    x_ref,
    traj_ref,
    cot_ref,
    init_ref,
    win_ref,
    wrec_ref,
    bias_ref,
    steps_ref,
    pairs_ref,
    quads_ref,
    sems,
):
    copies = [
        pltpu.make_async_copy(src, dst, sems.at[i])
        for i, (src, dst) in enumerate(
            (
                (traj_hbm, traj_ref),
                (wrec_hbm, wrec_ref),
                (init_hbm, init_ref),
                (x_hbm, x_ref),
                (win_hbm, win_ref),
                (bias_hbm, bias_ref),
                (cot_hbm, cot_ref),
            )
        )
    ]
    for copy in copies:
        copy.start()
    for copy in copies[:3]:
        copy.wait()
    traj = traj_ref[0]
    rec_in = jnp.concatenate([traj, pad8(init_ref[...])], axis=0)
    rec_all = jnp.dot(
        rec_in, wrec_ref[...], precision=lax.Precision.HIGHEST, preferred_element_type=F32
    )
    rec_init = rec_all[H : H + 1]
    rec_rows = rec_all[:H]
    for copy in copies[3:]:
        copy.wait()
    proj = (
        jnp.dot(x_ref[0], win_ref[...], precision=lax.Precision.HIGHEST, preferred_element_type=F32)
        + bias_ref[...].reshape(1, 3 * H)
    )
    rec = pltpu.roll(rec_rows, 1, 0)
    prev = pltpu.roll(traj, 1, 0)
    write, terms, off = gates(parts3(proj), parts3(rec), prev)
    inner = lax.broadcasted_iota(jnp.int32, (H, H), 0) > 0
    write = jnp.where(inner, write, 0.0)
    terms = [jnp.where(inner, t, 0.0) for t in terms]
    off = jnp.where(inner, off, 0.0)
    for p, rows in enumerate((*terms, write, off)):
        steps_ref[p] = rows
    save = pltpu.make_async_copy(steps_ref, steps_hbm, sems.at[7])
    save.start()

    ident = eye()
    per_block = H // BLOCKS
    u_side, u_back = weights_of(wrec_ref)

    def some_pairs(k, carry):
        fwd, bwd = carry
        base = pl.multiple_of(k * 16, 16)
        for half in range(2):
            rows = [steps_ref[p, pl.ds(base + 8 * half, 8), :] for p in range(4)]
            u = [wrec_ref[:, p * H : (p + 1) * H] for p in range(3)]
            for i in range(4):
                maps = []
                for l in (2 * i, 2 * i + 1):
                    row = [r[l : l + 1] for r in rows]
                    maps.append(leaf(u, row[3], row[:3], ident))
                pairs_ref[8 * k + 4 * half + i] = maps[0] + maps[1] + mm(*maps)
        fwd = forward_step(fwd, steps_ref, k, u_side, per_block)
        _, bwd = backward_step(bwd, steps_ref, cot_ref, per_block - 1 - k, u_back, per_block)
        return fwd, bwd

    zero = jnp.zeros((BLOCKS, H), F32)
    fwd, bwd = lax.fori_loop(0, 8, some_pairs, (zero, zero), unroll=8)
    for k in range(BLOCKS):
        nodes_ref[BLOCKS + k, H:] = two_rows(fwd[k : k + 1], bwd[k : k + 1])

    def joined(ref, i):
        early, late = ref[2 * i], ref[2 * i + 1]
        return early + late + mm(early, late)

    def some_quads(k, carry):
        for i in range(8):
            quads_ref[8 * k + i] = joined(pairs_ref, 8 * k + i)
        return carry

    lax.fori_loop(0, 4, some_quads, 0, unroll=4)

    def some_blocks(k, carry):
        for i in range(8):
            nodes_ref[BLOCKS + 8 * k + i, :H] = joined(quads_ref, 8 * k + i)
        return carry

    lax.fori_loop(0, 2, some_blocks, 0, unroll=2)

    def node(n):
        return nodes_ref[n, :H], nodes_ref[n, H : H + 1], nodes_ref[n, H + 1 : H + 2]

    for n in range(BLOCKS - 1, 0, -1):
        m, v, c = compose(node(2 * n), node(2 * n + 1))
        nodes_ref[n, :H] = m
        nodes_ref[n, H:] = two_rows(v, c)
    nodes_ref[0, :8] = jnp.concatenate(
        [*parts3(rec_init), init_ref[...], jnp.zeros((4, H), F32)], axis=0
    )
    nodes_ref[0, 8:] = jnp.zeros((H, H), F32)
    m, v, c = node(1)
    rec_last = rec_rows[H - 1 : H]
    write_pack(
        pack_ref,
        m,
        [v, c]
        + [proj[0:1, p * H : (p + 1) * H] for p in range(3)]
        + [rec_last[:, p * H : (p + 1) * H] for p in range(3)]
        + [traj[H - 1 : H]],
    )
    save.wait()


def two_rows(v, c):
    return jnp.concatenate([v, c, jnp.zeros((6, H), F32)], axis=0)


def write_pack(pack_ref, m, rows):
    tail = jnp.concatenate(rows + [jnp.zeros((ROWS - H - len(rows), H), F32)], axis=0)
    for i in range(pack_ref.shape[0]):
        pack_ref[i, :H] = m
        pack_ref[i, H:] = tail


def weights_of(wrec_ref):
    u = wrec_ref[...]
    return halves(u), halves(u.T)


def every(ref, l, per_block):
    return ref[pl.ds(l, BLOCKS, stride=per_block), :]


def forward_step(h, steps_ref, l, u_side, per_block):
    term = [every(steps_ref.at[p], l, per_block) for p in range(5)]
    mapped = parts3(few_rows(h, u_side))
    moved = term[0] * mapped[0] + term[1] * mapped[1] + term[2] * mapped[2]
    return h + (moved - term[3] * h) + term[4]


def backward_step(carried, steps_ref, cot_ref, l, u_back, per_block):
    term = [every(steps_ref.at[p], l, per_block) for p in range(4)]
    costate = carried + every(cot_ref.at[0], l, per_block)
    scaled = jnp.concatenate([term[p] * costate for p in range(3)], axis=1)
    back = few_rows(scaled, u_back)
    return costate, costate + (back - term[3] * costate)


def boundaries(group_ref, wrec_ref, ident):
    u = [wrec_ref[:, p * H : (p + 1) * H] for p in range(3)]
    found = []
    for j in range(1, 4):
        proj = [group_ref[j, ROW_PROJ + p : ROW_PROJ + p + 1] for p in range(3)]
        rec = [group_ref[j - 1, ROW_REC + p : ROW_REC + p + 1] for p in range(3)]
        write, terms, off = gates(proj, rec, group_ref[j - 1, ROW_LAST : ROW_LAST + 1])
        found.append((leaf(u, write, terms, ident), off))
    return found


def links(group_ref, wrec_ref):
    ident = eye()
    firsts = boundaries(group_ref, wrec_ref, ident)
    ahead, behind = [], []
    for j in range(3):
        first, off = firsts[j]
        part = group_ref[j, :H]
        prod = mm(group_ref[j, : H + 8], first)
        ahead.append(
            (
                part + first + prod[:H],
                group_ref[j, ROW_B : ROW_B + 1] + off + prod[ROW_B : ROW_B + 1],
            )
        )
        part = group_ref[j + 1, :H]
        cc = group_ref[j + 1, ROW_C : ROW_C + 1]
        prod = mm(jnp.concatenate([first, pad8(off)], axis=0), part)
        behind.append(
            (
                part + first + prod[:H],
                off + prod[H : H + 1] + group_ref[j + 1, ROW_B : ROW_B + 1],
                cc + vec_mm_t(cc, first),
            )
        )
    return ahead, behind


def merge_kernel(group_ref, wrec_ref, pack_ref, links_ref):
    ahead, behind = links(group_ref, wrec_ref)
    for j in range(3):
        m, v = ahead[j]
        links_ref[j, :H] = m
        links_ref[j, H:] = pad8(v)
        m, v, c = behind[j]
        links_ref[3 + j, :H] = m
        links_ref[3 + j, H:] = pad8(c)
    start = (
        group_ref[0, :H],
        group_ref[0, ROW_B : ROW_B + 1],
        group_ref[0, ROW_C : ROW_C + 1],
    )
    m, v, c = compose(compose(start, behind[0]), compose(behind[1], behind[2]))
    write_pack(
        pack_ref,
        m,
        [v, c]
        + [group_ref[0, ROW_PROJ + p : ROW_PROJ + p + 1] for p in range(3)]
        + [group_ref[3, ROW_REC + p : ROW_REC + p + 1] for p in range(3)]
        + [group_ref[3, ROW_LAST : ROW_LAST + 1]],
    )


def places():
    place = lax.axis_index("seq")
    return place // 16, place % 4


def forward_join(early, late):
    prod = mm(jnp.concatenate([early[0], pad8(early[1])], axis=0), late[0])
    return early[0] + late[0] + prod[:H], early[1] + late[1] + prod[H : H + 1]


def adjoint_join(early, late):
    return (
        early[0] + late[0] + mm(early[0], late[0]),
        early[1] + late[1] + vec_mm_t(late[1], early[0]),
    )


def paths_to(own, links_ref):
    ahead = [(links_ref[j, :H], links_ref[j, H : H + 1]) for j in range(3)]
    behind = [(links_ref[3 + j, :H], links_ref[3 + j, H : H + 1]) for j in range(3)]
    keep = lambda on, new, old: tuple(jnp.where(on, n, o) for n, o in zip(new, old))
    none = (jnp.zeros((H, H), F32), jnp.zeros((1, H), F32))
    to = keep(own > 0, ahead[0], none)
    back = keep(own < 3, behind[2], none)
    for j in (1, 2):
        to = keep(own > j, forward_join(to, ahead[j]), to)
        back = keep(own < 3 - j, adjoint_join(behind[2 - j], back), back)
    return to, back


def pair_kernel(own_ref, other_ref, wrec_ref, pack_ref, path_ref, *, bit):
    second = lax.axis_index("seq") // bit % 2 == 1
    own, other = own_ref[0], other_ref[0]
    early = jnp.where(second, other, own)
    late = jnp.where(second, own, other)
    u = [wrec_ref[:, p * H : (p + 1) * H] for p in range(3)]
    write, terms, off = gates(
        [late[ROW_PROJ + p : ROW_PROJ + p + 1] for p in range(3)],
        [early[ROW_REC + p : ROW_REC + p + 1] for p in range(3)],
        early[ROW_LAST : ROW_LAST + 1],
    )
    first = leaf(u, write, terms, eye())
    early_v, early_c = early[ROW_B : ROW_B + 1], early[ROW_C : ROW_C + 1]
    late_v, late_c = late[ROW_B : ROW_B + 1], late[ROW_C : ROW_C + 1]
    ahead = forward_join((early[:H], early_v), (first, off))
    prod = mm(jnp.concatenate([first, pad8(off)], axis=0), late[:H])
    behind = (
        first + late[:H] + prod[:H],
        off + prod[H : H + 1] + late_v,
        late_c + vec_mm_t(late_c, first),
    )
    path_ref[0, :H] = jnp.where(second, ahead[0], 0.0)
    path_ref[0, H:] = pad8(jnp.where(second, ahead[1], 0.0))
    path_ref[1, :H] = jnp.where(second, 0.0, behind[0])
    path_ref[1, H:] = pad8(jnp.where(second, 0.0, behind[2]))
    m, v, c = compose((early[:H], early_v, early_c), behind)
    write_pack(
        pack_ref,
        m,
        [v, c]
        + [early[ROW_PROJ + p : ROW_PROJ + p + 1] for p in range(3)]
        + [late[ROW_REC + p : ROW_REC + p + 1] for p in range(3)]
        + [late[ROW_LAST : ROW_LAST + 1]],
    )


def reach_kernel(
    links1_ref,
    path2_ref,
    path3_ref,
    wrec_ref,
    maps_hbm,
    vecs_hbm,
    u_hbm,
    ut_hbm,
    maps_ref,
    vecs_ref,
    u_ref,
    ut_ref,
    sems,
):
    to, back = paths_to(places()[1], links1_ref)
    for path_ref in (path2_ref, path3_ref):
        to = forward_join((path_ref[0, :H], path_ref[0, H : H + 1]), to)
        back = adjoint_join(back, (path_ref[1, :H], path_ref[1, H : H + 1]))

    def put(slot, found, flip):
        m, v = found
        maps_ref[slot] = halves(m.T if flip else m)
        vecs_ref[slot : slot + 1] = v

    put(0, to, False)
    put(1, back, True)
    vecs_ref[2:] = jnp.zeros((6, H), F32)
    u = wrec_ref[...]
    u_ref[...] = halves(u)
    ut_ref[...] = halves(u.T)
    copies = [
        pltpu.make_async_copy(src, dst, sems.at[i])
        for i, (src, dst) in enumerate(
            ((maps_ref, maps_hbm), (vecs_ref, vecs_hbm), (u_ref, u_hbm), (ut_ref, ut_hbm))
        )
    ]
    for copy in copies:
        copy.start()
    for copy in copies:
        copy.wait()


def moved_by(vector, weights):
    return few_rows(pad8(vector), weights)[:1]


def apply_kernel(
    group_ref,
    nodes_ref,
    wrec_ref,
    maps_hbm,
    vecs_hbm,
    u_hbm,
    ut_hbm,
    steps_hbm,
    cot_hbm,
    state_ref,
    adjoint_ref,
    maps_ref,
    vecs_ref,
    u_ref,
    ut_ref,
    steps_ref,
    cot_ref,
    sems,
):
    copies = [
        pltpu.make_async_copy(src, dst, sems.at[i])
        for i, (src, dst) in enumerate(
            (
                (maps_hbm, maps_ref),
                (vecs_hbm, vecs_ref),
                (u_hbm, u_ref),
                (ut_hbm, ut_ref),
                (steps_hbm, steps_ref),
                (cot_hbm, cot_ref),
            )
        )
    ]
    for copy in copies:
        copy.start()
    per_block = H // BLOCKS
    ahead, behind = links(group_ref, wrec_ref)
    init = nodes_ref[0, 3:4]
    rec = [nodes_ref[0, p : p + 1] for p in range(3)]
    write, terms, off = gates(
        [group_ref[0, ROW_PROJ + p : ROW_PROJ + p + 1] for p in range(3)], rec, init
    )
    state = (
        init
        + (terms[0] * rec[0] + terms[1] * rec[1] + terms[2] * rec[2])
        - write * init
        + off
    )
    costate = jnp.zeros((1, H), F32)
    own = places()[0]
    for j in range(3):
        moved = state + vec_mm(state, ahead[j][0]) + ahead[j][1]
        state = jnp.where(j < own, moved, state)
        i = 2 - j
        moved = costate + vec_mm_t(costate, behind[i][0]) + behind[i][2]
        costate = jnp.where(i >= own, moved, costate)
    for copy in copies[:2]:
        copy.wait()
    states = {1: state + moved_by(state, maps_ref[0]) + vecs_ref[0:1]}
    costates = {1: costate + moved_by(costate, maps_ref[1]) + vecs_ref[1:2]}
    for n in range(1, BLOCKS):
        state, costate = states[n], costates[n]
        states[2 * n] = state
        states[2 * n + 1] = (
            state + vec_mm(state, nodes_ref[2 * n, :H]) + nodes_ref[2 * n, H : H + 1]
        )
        costates[2 * n] = (
            costate
            + vec_mm_t(costate, nodes_ref[2 * n + 1, :H])
            + nodes_ref[2 * n + 1, H + 1 : H + 2]
        )
        costates[2 * n + 1] = costate
    fwd = jnp.concatenate([states[BLOCKS + k] for k in range(BLOCKS)], axis=0)
    bwd = jnp.concatenate([costates[BLOCKS + k] for k in range(BLOCKS)], axis=0)
    for copy in copies[2:]:
        copy.wait()
    u_side, u_back = u_ref[...], ut_ref[...]
    for l in range(per_block):
        fwd = forward_step(fwd, steps_ref, l, u_side, per_block)
        state_ref.at[0][pl.ds(l, BLOCKS, stride=per_block), :] = fwd
        back = per_block - 1 - l
        out, bwd = backward_step(bwd, steps_ref, cot_ref, back, u_back, per_block)
        adjoint_ref.at[0][pl.ds(back, BLOCKS, stride=per_block), :] = out


def call(kernel, out_shape, flops, spaces, outs, scratch=()):
    kinds = {"s": pltpu.SMEM, "v": pltpu.VMEM, "h": pltpu.HBM}
    run = pl.pallas_call(
        kernel,
        out_shape=tuple(
            pltpu.HBM(o.shape, o.dtype) if k == "h" else o for k, o in zip(outs, out_shape)
        ),
        in_specs=[pl.BlockSpec(memory_space=kinds[k]) for k in spaces],
        out_specs=tuple(pl.BlockSpec(memory_space=kinds[k]) for k in outs),
        scratch_shapes=list(scratch),
        compiler_params=pltpu.CompilerParams(vmem_limit_bytes=VMEM_LIMIT),
        cost_estimate=pl.CostEstimate(flops=flops, bytes_accessed=2**20, transcendentals=0),
    )

    def placed(*args):
        return run(
            *(
                pltpu.with_memory_space_constraint(a, pltpu.HBM) if k == "h" else a
                for k, a in zip(spaces, args)
            )
        )

    return placed


def group_lists(count):
    near = [list(range(s, s + 4)) for s in range(0, count, 4)]
    far = [[16 * y + z for y in range(4)] for z in range(16)]
    return near, far


def shape(*dims):
    return jax.ShapeDtypeStruct(dims, F32)


def per_device(
    inputs, trajectory, initial_state, cotangent, in_weight, recurrent_weight, gate_bias
):
    count = lax.axis_size("seq")
    near, far = group_lists(count)
    pack, nodes, steps = call(
        local_kernel,
        (
            shape(4, ROWS, H),
            shape(2 * BLOCKS, H + 8, H),
            shape(5, H, H),
        ),
        2 * 10**9,
        "hhhhhhh",
        "vvh",
        [
            pltpu.VMEM((1, H, H), F32),
            pltpu.VMEM((1, H, H), F32),
            pltpu.VMEM((1, H, H), F32),
            pltpu.VMEM((1, H), F32),
            pltpu.VMEM((H, 3 * H), F32),
            pltpu.VMEM((H, 3 * H), F32),
            pltpu.VMEM((3 * H,), F32),
            pltpu.VMEM((5, H, H), F32),
            pltpu.VMEM((64, H, H), F32),
            pltpu.VMEM((32, H, H), F32),
            pltpu.SemaphoreType.DMA((8,)),
        ],
    )(
        inputs,
        trajectory,
        cotangent,
        initial_state,
        in_weight,
        recurrent_weight,
        gate_bias,
    )
    merge = call(
        merge_kernel, (shape(1, ROWS, H), shape(6, H + 8, H)), 10**8, "vv", "vv"
    )

    def exchange(packed, groups):
        return lax.all_to_all(packed, "seq", 0, 0, axis_index_groups=groups)

    def pair(packed, bit, flip, copies):
        other = lax.ppermute(packed, "seq", [(i, i ^ flip) for i in range(count)])
        return call(
            functools.partial(pair_kernel, bit=bit),
            (shape(copies, ROWS, H), shape(2, H + 8, H)),
            10**8,
            "vvv",
            "vv",
        )(packed, other, recurrent_weight)

    pack, links1 = merge(exchange(pack, near), recurrent_weight)
    pack, path2 = pair(pack, 4, 7, 1)
    pack, path3 = pair(pack, 8, 12, 4)
    group = exchange(pack, far)
    found = (
        (2, H, 2 * H),
        (8, H),
        (H, 6 * H),
        (3 * H, 2 * H),
    )
    kinds = (BF16, F32, BF16, BF16)
    buffers = [pltpu.VMEM(dims, kind) for dims, kind in zip(found, kinds)]
    reached = call(
        reach_kernel,
        tuple(jax.ShapeDtypeStruct(dims, kind) for dims, kind in zip(found, kinds)),
        10**8,
        "vvvv",
        "hhhh",
        buffers + [pltpu.SemaphoreType.DMA((4,))],
    )(links1, path2, path3, recurrent_weight)
    new_state, adjoint = call(
        apply_kernel,
        (shape(1, H, H), shape(1, H, H)),
        10**8,
        "vvvhhhhhh",
        "vv",
        buffers
        + [
            pltpu.VMEM((5, H, H), F32),
            pltpu.VMEM((1, H, H), F32),
            pltpu.SemaphoreType.DMA((6,)),
        ],
    )(group, nodes, recurrent_weight, *reached, steps, cotangent)
    return new_state, adjoint


def solution(mesh):
    return jax.shard_map(
        per_device,
        mesh=mesh,
        in_specs=(
            P("dp", "seq", None),
            P("dp", "seq", None),
            P("dp", None),
            P("dp", "seq", None),
            P(),
            P(),
            P(),
        ),
        out_specs=(P("dp", "seq", None), P("dp", "seq", None)),
        check_vma=False,
    )
```

```python
import functools

import jax
import jax.numpy as jnp
from jax import lax
from jax.experimental import pallas as pl
from jax.experimental.pallas import tpu as pltpu
from jax.sharding import PartitionSpec as P

F32 = jnp.float32
BF16 = jnp.bfloat16
H = 128
BLOCKS = 16
ROW_B = 128
ROW_C = 129
ROW_PROJ = 130
ROW_REC = 133
ROW_LAST = 136
ROWS = 144
VMEM_LIMIT = 24 * 1024 * 1024


def split(x):
    hi = x.astype(BF16)
    return hi, (x - hi.astype(F32)).astype(BF16)


def left(x):
    return jnp.concatenate(split(x), axis=1)


def right(x):
    row = jnp.concatenate(split(x), axis=1)
    return jnp.concatenate([row, row], axis=0)


def both_halves(out):
    half = out.shape[1] // 2
    return out[:, :half] + out[:, half:]


def mm(a, b):
    return both_halves(jnp.dot(left(a), right(b), preferred_element_type=F32))


def pad8(row):
    return jnp.broadcast_to(row, (8, H))


def halves(x):
    return jnp.concatenate(split(x), axis=1)


def stacked(x):
    return jnp.concatenate(split(x), axis=0)


def few_rows(x, weights):
    out = jnp.dot(stacked(x), weights, preferred_element_type=F32)
    return both_halves(out[: x.shape[0]] + out[x.shape[0] :])


def vec_mm(row, b):
    return few_rows(pad8(row), halves(b))[:1]


def vec_mm_t(row, b):
    out = lax.dot_general(
        stacked(pad8(row)), stacked(b), (((1,), (1,)), ((), ())), preferred_element_type=F32
    )
    return both_halves(out[:8] + out[8:])[:1]


def eye():
    rows = lax.broadcasted_iota(jnp.int32, (H, H), 0)
    cols = lax.broadcasted_iota(jnp.int32, (H, H), 1)
    return (rows == cols).astype(F32)


def gates(proj, rec, prev):
    reset = jax.nn.sigmoid(proj[0] + rec[0])
    write = jax.nn.sigmoid(proj[1] + rec[1])
    cand = jnp.tanh(proj[2] + reset * rec[2])
    slope = write * (1.0 - cand * cand)
    terms = (
        slope * rec[2] * reset * (1.0 - reset),
        (cand - prev) * write * (1.0 - write),
        slope * reset,
    )
    off = write * cand - (terms[0] * rec[0] + terms[1] * rec[1] + terms[2] * rec[2])
    return write, terms, off


def parts3(x):
    return x[:, :H], x[:, H : 2 * H], x[:, 2 * H :]


def leaf(u, write, terms, ident):
    return u[0] * terms[0] + u[1] * terms[1] + u[2] * terms[2] - ident * write


def compose(early, late):
    lb, lv, lc = early
    rb, rv, rc = late
    prod = mm(jnp.concatenate([lb, pad8(lv)], axis=0), rb)
    return (
        lb + rb + prod[:H],
        lv + rv + prod[H : H + 1],
        lc + rc + vec_mm_t(rc, lb),
    )


def local_kernel(
    x_hbm,
    traj_hbm,
    cot_hbm,
    init_hbm,
    win_hbm,
    wrec_hbm,
    bias_hbm,
    pack_ref,
    nodes_ref,
    steps_hbm,
    x_ref,
    traj_ref,
    cot_ref,
    init_ref,
    win_ref,
    wrec_ref,
    bias_ref,
    steps_ref,
    pairs_ref,
    quads_ref,
    sems,
):
    copies = [
        pltpu.make_async_copy(src, dst, sems.at[i])
        for i, (src, dst) in enumerate(
            (
                (traj_hbm, traj_ref),
                (wrec_hbm, wrec_ref),
                (init_hbm, init_ref),
                (x_hbm, x_ref),
                (win_hbm, win_ref),
                (bias_hbm, bias_ref),
                (cot_hbm, cot_ref),
            )
        )
    ]
    for copy in copies:
        copy.start()
    for copy in copies[:3]:
        copy.wait()
    traj = traj_ref[0]
    rec_in = jnp.concatenate([traj, pad8(init_ref[...])], axis=0)
    rec_all = jnp.dot(
        rec_in, wrec_ref[...], precision=lax.Precision.HIGHEST, preferred_element_type=F32
    )
    rec_init = rec_all[H : H + 1]
    rec_rows = rec_all[:H]
    for copy in copies[3:]:
        copy.wait()
    proj = (
        jnp.dot(x_ref[0], win_ref[...], precision=lax.Precision.HIGHEST, preferred_element_type=F32)
        + bias_ref[...].reshape(1, 3 * H)
    )
    rec = pltpu.roll(rec_rows, 1, 0)
    prev = pltpu.roll(traj, 1, 0)
    write, terms, off = gates(parts3(proj), parts3(rec), prev)
    inner = lax.broadcasted_iota(jnp.int32, (H, H), 0) > 0
    write = jnp.where(inner, write, 0.0)
    terms = [jnp.where(inner, t, 0.0) for t in terms]
    off = jnp.where(inner, off, 0.0)
    for p, rows in enumerate((*terms, write, off)):
        steps_ref[p] = rows
    save = pltpu.make_async_copy(steps_ref, steps_hbm, sems.at[7])
    save.start()

    ident = eye()
    per_block = H // BLOCKS
    u_side, u_back = weights_of(wrec_ref)

    def some_pairs(k, carry):
        fwd, bwd = carry
        base = pl.multiple_of(k * 16, 16)
        for half in range(2):
            rows = [steps_ref[p, pl.ds(base + 8 * half, 8), :] for p in range(4)]
            u = [wrec_ref[:, p * H : (p + 1) * H] for p in range(3)]
            for i in range(4):
                maps = []
                for l in (2 * i, 2 * i + 1):
                    row = [r[l : l + 1] for r in rows]
                    maps.append(leaf(u, row[3], row[:3], ident))
                pairs_ref[8 * k + 4 * half + i] = maps[0] + maps[1] + mm(*maps)
        fwd = forward_step(fwd, steps_ref, k, u_side, per_block)
        _, bwd = backward_step(bwd, steps_ref, cot_ref, per_block - 1 - k, u_back, per_block)
        return fwd, bwd

    zero = jnp.zeros((BLOCKS, H), F32)
    fwd, bwd = lax.fori_loop(0, 8, some_pairs, (zero, zero), unroll=8)
    for k in range(BLOCKS):
        nodes_ref[BLOCKS + k, H:] = two_rows(fwd[k : k + 1], bwd[k : k + 1])

    def joined(ref, i):
        early, late = ref[2 * i], ref[2 * i + 1]
        return early + late + mm(early, late)

    def some_quads(k, carry):
        for i in range(8):
            quads_ref[8 * k + i] = joined(pairs_ref, 8 * k + i)
        return carry

    lax.fori_loop(0, 4, some_quads, 0, unroll=4)

    def some_blocks(k, carry):
        for i in range(8):
            nodes_ref[BLOCKS + 8 * k + i, :H] = joined(quads_ref, 8 * k + i)
        return carry

    lax.fori_loop(0, 2, some_blocks, 0, unroll=2)

    def node(n):
        return nodes_ref[n, :H], nodes_ref[n, H : H + 1], nodes_ref[n, H + 1 : H + 2]

    for n in range(BLOCKS - 1, 0, -1):
        m, v, c = compose(node(2 * n), node(2 * n + 1))
        nodes_ref[n, :H] = m
        nodes_ref[n, H:] = two_rows(v, c)
    nodes_ref[0, :8] = jnp.concatenate(
        [*parts3(rec_init), init_ref[...], jnp.zeros((4, H), F32)], axis=0
    )
    nodes_ref[0, 8:] = jnp.zeros((H, H), F32)
    m, v, c = node(1)
    rec_last = rec_rows[H - 1 : H]
    write_pack(
        pack_ref,
        m,
        [v, c]
        + [proj[0:1, p * H : (p + 1) * H] for p in range(3)]
        + [rec_last[:, p * H : (p + 1) * H] for p in range(3)]
        + [traj[H - 1 : H]],
    )
    save.wait()


def two_rows(v, c):
    return jnp.concatenate([v, c, jnp.zeros((6, H), F32)], axis=0)


def write_pack(pack_ref, m, rows):
    tail = jnp.concatenate(rows + [jnp.zeros((ROWS - H - len(rows), H), F32)], axis=0)
    for i in range(pack_ref.shape[0]):
        pack_ref[i, :H] = m
        pack_ref[i, H:] = tail


def weights_of(wrec_ref):
    u = wrec_ref[...]
    return halves(u), halves(u.T)


def every(ref, l, per_block):
    return ref[pl.ds(l, BLOCKS, stride=per_block), :]


def forward_step(h, steps_ref, l, u_side, per_block):
    term = [every(steps_ref.at[p], l, per_block) for p in range(5)]
    mapped = parts3(few_rows(h, u_side))
    moved = term[0] * mapped[0] + term[1] * mapped[1] + term[2] * mapped[2]
    return h + (moved - term[3] * h) + term[4]


def backward_step(carried, steps_ref, cot_ref, l, u_back, per_block):
    term = [every(steps_ref.at[p], l, per_block) for p in range(4)]
    costate = carried + every(cot_ref.at[0], l, per_block)
    scaled = jnp.concatenate([term[p] * costate for p in range(3)], axis=1)
    back = few_rows(scaled, u_back)
    return costate, costate + (back - term[3] * costate)


def boundaries(group_ref, wrec_ref, ident):
    u = [wrec_ref[:, p * H : (p + 1) * H] for p in range(3)]
    found = []
    for j in range(1, 4):
        proj = [group_ref[j, ROW_PROJ + p : ROW_PROJ + p + 1] for p in range(3)]
        rec = [group_ref[j - 1, ROW_REC + p : ROW_REC + p + 1] for p in range(3)]
        write, terms, off = gates(proj, rec, group_ref[j - 1, ROW_LAST : ROW_LAST + 1])
        found.append((leaf(u, write, terms, ident), off))
    return found


def links(group_ref, wrec_ref):
    ident = eye()
    firsts = boundaries(group_ref, wrec_ref, ident)
    ahead, behind = [], []
    for j in range(3):
        first, off = firsts[j]
        part = group_ref[j, :H]
        prod = mm(group_ref[j, : H + 8], first)
        ahead.append(
            (
                part + first + prod[:H],
                group_ref[j, ROW_B : ROW_B + 1] + off + prod[ROW_B : ROW_B + 1],
            )
        )
        part = group_ref[j + 1, :H]
        cc = group_ref[j + 1, ROW_C : ROW_C + 1]
        prod = mm(jnp.concatenate([first, pad8(off)], axis=0), part)
        behind.append(
            (
                part + first + prod[:H],
                off + prod[H : H + 1] + group_ref[j + 1, ROW_B : ROW_B + 1],
                cc + vec_mm_t(cc, first),
            )
        )
    return ahead, behind


def merge_kernel(group_ref, wrec_ref, pack_ref, path_ref):
    ahead, behind = links(group_ref, wrec_ref)
    put_path(path_ref, *paths_to(places()[1], ahead, [(m, c) for m, _, c in behind]))
    start = (
        group_ref[0, :H],
        group_ref[0, ROW_B : ROW_B + 1],
        group_ref[0, ROW_C : ROW_C + 1],
    )
    m, v, c = compose(compose(start, behind[0]), compose(behind[1], behind[2]))
    write_pack(
        pack_ref,
        m,
        [v, c]
        + [group_ref[0, ROW_PROJ + p : ROW_PROJ + p + 1] for p in range(3)]
        + [group_ref[3, ROW_REC + p : ROW_REC + p + 1] for p in range(3)]
        + [group_ref[3, ROW_LAST : ROW_LAST + 1]],
    )


def places():
    place = lax.axis_index("seq")
    return place // 16, place % 4


def forward_join(early, late):
    prod = mm(jnp.concatenate([early[0], pad8(early[1])], axis=0), late[0])
    return early[0] + late[0] + prod[:H], early[1] + late[1] + prod[H : H + 1]


def adjoint_join(early, late):
    return (
        early[0] + late[0] + mm(early[0], late[0]),
        early[1] + late[1] + vec_mm_t(late[1], early[0]),
    )


def paths_to(own, ahead, behind):
    keep = lambda on, new, old: tuple(jnp.where(on, n, o) for n, o in zip(new, old))
    none = (jnp.zeros((H, H), F32), jnp.zeros((1, H), F32))
    to = keep(own > 0, ahead[0], none)
    back = keep(own < 3, behind[2], none)
    for j in (1, 2):
        to = keep(own > j, forward_join(to, ahead[j]), to)
        back = keep(own < 3 - j, adjoint_join(behind[2 - j], back), back)
    return to, back


def put_path(path_ref, to, back):
    for i, (m, v) in enumerate((to, back)):
        path_ref[i, :H] = m
        path_ref[i, H:] = pad8(v)


def pair_kernel(own_ref, other_ref, inner_ref, wrec_ref, pack_ref, path_ref, *, bit):
    second = lax.axis_index("seq") // bit % 2 == 1
    own, other = own_ref[0], other_ref[0]
    early = jnp.where(second, other, own)
    late = jnp.where(second, own, other)
    u = [wrec_ref[:, p * H : (p + 1) * H] for p in range(3)]
    write, terms, off = gates(
        [late[ROW_PROJ + p : ROW_PROJ + p + 1] for p in range(3)],
        [early[ROW_REC + p : ROW_REC + p + 1] for p in range(3)],
        early[ROW_LAST : ROW_LAST + 1],
    )
    first = leaf(u, write, terms, eye())
    early_v, early_c = early[ROW_B : ROW_B + 1], early[ROW_C : ROW_C + 1]
    late_v, late_c = late[ROW_B : ROW_B + 1], late[ROW_C : ROW_C + 1]
    ahead = forward_join((early[:H], early_v), (first, off))
    prod = mm(jnp.concatenate([first, pad8(off)], axis=0), late[:H])
    behind = (
        first + late[:H] + prod[:H],
        off + prod[H : H + 1] + late_v,
        late_c + vec_mm_t(late_c, first),
    )
    to = tuple(jnp.where(second, a, 0.0) for a in ahead)
    back = tuple(jnp.where(second, 0.0, a) for a in (behind[0], behind[2]))
    put_path(
        path_ref,
        forward_join(to, (inner_ref[0, :H], inner_ref[0, H : H + 1])),
        adjoint_join((inner_ref[1, :H], inner_ref[1, H : H + 1]), back),
    )
    m, v, c = compose((early[:H], early_v, early_c), behind)
    write_pack(
        pack_ref,
        m,
        [v, c]
        + [early[ROW_PROJ + p : ROW_PROJ + p + 1] for p in range(3)]
        + [late[ROW_REC + p : ROW_REC + p + 1] for p in range(3)]
        + [late[ROW_LAST : ROW_LAST + 1]],
    )


def apply_kernel(
    group_ref,
    path_ref,
    nodes_ref,
    wrec_ref,
    steps_hbm,
    cot_hbm,
    state_ref,
    adjoint_ref,
    steps_ref,
    cot_ref,
    sems,
):
    copies = [
        pltpu.make_async_copy(steps_hbm, steps_ref, sems.at[0]),
        pltpu.make_async_copy(cot_hbm, cot_ref, sems.at[1]),
    ]
    for copy in copies:
        copy.start()
    per_block = H // BLOCKS
    ahead, behind = links(group_ref, wrec_ref)
    init = nodes_ref[0, 3:4]
    rec = [nodes_ref[0, p : p + 1] for p in range(3)]
    write, terms, off = gates(
        [group_ref[0, ROW_PROJ + p : ROW_PROJ + p + 1] for p in range(3)], rec, init
    )
    state = (
        init
        + (terms[0] * rec[0] + terms[1] * rec[1] + terms[2] * rec[2])
        - write * init
        + off
    )
    costate = jnp.zeros((1, H), F32)
    own = places()[0]
    for j in range(3):
        moved = state + vec_mm(state, ahead[j][0]) + ahead[j][1]
        state = jnp.where(j < own, moved, state)
        i = 2 - j
        moved = costate + vec_mm(costate, behind[i][0].T) + behind[i][2]
        costate = jnp.where(i >= own, moved, costate)
    states = {1: state + vec_mm(state, path_ref[0, :H]) + path_ref[0, H : H + 1]}
    costates = {1: costate + vec_mm(costate, path_ref[1, :H].T) + path_ref[1, H : H + 1]}
    for n in range(1, BLOCKS):
        state, costate = states[n], costates[n]
        states[2 * n] = state
        states[2 * n + 1] = (
            state + vec_mm(state, nodes_ref[2 * n, :H]) + nodes_ref[2 * n, H : H + 1]
        )
        costates[2 * n] = (
            costate
            + vec_mm(costate, nodes_ref[2 * n + 1, :H].T)
            + nodes_ref[2 * n + 1, H + 1 : H + 2]
        )
        costates[2 * n + 1] = costate
    fwd = jnp.concatenate([states[BLOCKS + k] for k in range(BLOCKS)], axis=0)
    bwd = jnp.concatenate([costates[BLOCKS + k] for k in range(BLOCKS)], axis=0)
    for copy in copies:
        copy.wait()
    u_side, u_back = weights_of(wrec_ref)
    for l in range(per_block):
        fwd = forward_step(fwd, steps_ref, l, u_side, per_block)
        state_ref.at[0][pl.ds(l, BLOCKS, stride=per_block), :] = fwd
        back = per_block - 1 - l
        out, bwd = backward_step(bwd, steps_ref, cot_ref, back, u_back, per_block)
        adjoint_ref.at[0][pl.ds(back, BLOCKS, stride=per_block), :] = out


def call(kernel, out_shape, flops, spaces, outs, scratch=()):
    kinds = {"s": pltpu.SMEM, "v": pltpu.VMEM, "h": pltpu.HBM}
    run = pl.pallas_call(
        kernel,
        out_shape=tuple(
            pltpu.HBM(o.shape, o.dtype) if k == "h" else o for k, o in zip(outs, out_shape)
        ),
        in_specs=[pl.BlockSpec(memory_space=kinds[k]) for k in spaces],
        out_specs=tuple(pl.BlockSpec(memory_space=kinds[k]) for k in outs),
        scratch_shapes=list(scratch),
        compiler_params=pltpu.CompilerParams(vmem_limit_bytes=VMEM_LIMIT),
        cost_estimate=pl.CostEstimate(flops=flops, bytes_accessed=2**20, transcendentals=0),
    )

    def placed(*args):
        return run(
            *(
                pltpu.with_memory_space_constraint(a, pltpu.HBM) if k == "h" else a
                for k, a in zip(spaces, args)
            )
        )

    return placed


def group_lists(count):
    near = [list(range(s, s + 4)) for s in range(0, count, 4)]
    far = [[16 * y + z for y in range(4)] for z in range(16)]
    return near, far


def shape(*dims):
    return jax.ShapeDtypeStruct(dims, F32)


def per_device(
    inputs, trajectory, initial_state, cotangent, in_weight, recurrent_weight, gate_bias
):
    count = lax.axis_size("seq")
    near, far = group_lists(count)
    pack, nodes, steps = call(
        local_kernel,
        (
            shape(4, ROWS, H),
            shape(2 * BLOCKS, H + 8, H),
            shape(5, H, H),
        ),
        2 * 10**9,
        "hhhhhhh",
        "vvh",
        [
            pltpu.VMEM((1, H, H), F32),
            pltpu.VMEM((1, H, H), F32),
            pltpu.VMEM((1, H, H), F32),
            pltpu.VMEM((1, H), F32),
            pltpu.VMEM((H, 3 * H), F32),
            pltpu.VMEM((H, 3 * H), F32),
            pltpu.VMEM((3 * H,), F32),
            pltpu.VMEM((5, H, H), F32),
            pltpu.VMEM((64, H, H), F32),
            pltpu.VMEM((32, H, H), F32),
            pltpu.SemaphoreType.DMA((8,)),
        ],
    )(
        inputs,
        trajectory,
        cotangent,
        initial_state,
        in_weight,
        recurrent_weight,
        gate_bias,
    )
    merge = call(
        merge_kernel, (shape(1, ROWS, H), shape(2, H + 8, H)), 10**8, "vv", "vv"
    )

    def exchange(packed, groups):
        return lax.all_to_all(packed, "seq", 0, 0, axis_index_groups=groups)

    def pair(packed, path, bit, flip, copies):
        other = lax.ppermute(packed, "seq", [(i, i ^ flip) for i in range(count)])
        return call(
            functools.partial(pair_kernel, bit=bit),
            (shape(copies, ROWS, H), shape(2, H + 8, H)),
            10**8,
            "vvvv",
            "vv",
        )(packed, other, path, recurrent_weight)

    pack, path = merge(exchange(pack, near), recurrent_weight)
    pack, path = pair(pack, path, 4, 7, 1)
    pack, path = pair(pack, path, 8, 12, 4)
    new_state, adjoint = call(
        apply_kernel,
        (shape(1, H, H), shape(1, H, H)),
        10**8,
        "vvvvhh",
        "vv",
        [
            pltpu.VMEM((5, H, H), F32),
            pltpu.VMEM((1, H, H), F32),
            pltpu.SemaphoreType.DMA((2,)),
        ],
    )(exchange(pack, far), path, nodes, recurrent_weight, steps, cotangent)
    return new_state, adjoint


def solution(mesh):
    return jax.shard_map(
        per_device,
        mesh=mesh,
        in_specs=(
            P("dp", "seq", None),
            P("dp", "seq", None),
            P("dp", None),
            P("dp", "seq", None),
            P(),
            P(),
            P(),
        ),
        out_specs=(P("dp", "seq", None), P("dp", "seq", None)),
        check_vma=False,
    )
```

```python
import functools

import jax
import jax.numpy as jnp
from jax import lax
from jax.experimental import pallas as pl
from jax.experimental.pallas import tpu as pltpu
from jax.sharding import PartitionSpec as P

F32 = jnp.float32
BF16 = jnp.bfloat16
H = 128
BLOCKS = 16
ROW_B = 128
ROW_C = 129
ROW_PROJ = 130
ROW_REC = 133
ROW_LAST = 136
ROWS = 144
VMEM_LIMIT = 24 * 1024 * 1024


def split(x):
    hi = x.astype(BF16)
    return hi, (x - hi.astype(F32)).astype(BF16)


def left(x):
    return jnp.concatenate(split(x), axis=1)


def right(x):
    row = jnp.concatenate(split(x), axis=1)
    return jnp.concatenate([row, row], axis=0)


def both_halves(out):
    half = out.shape[1] // 2
    return out[:, :half] + out[:, half:]


def mm(a, b):
    return both_halves(jnp.dot(left(a), right(b), preferred_element_type=F32))


def pad8(row):
    return jnp.broadcast_to(row, (8, H))


def halves(x):
    return jnp.concatenate(split(x), axis=1)


def stacked(x):
    return jnp.concatenate(split(x), axis=0)


def few_rows(x, weights):
    out = jnp.dot(stacked(x), weights, preferred_element_type=F32)
    return both_halves(out[: x.shape[0]] + out[x.shape[0] :])


def vec_mm(row, b):
    return few_rows(pad8(row), halves(b))[:1]


def vec_mm_t(row, b):
    out = lax.dot_general(
        stacked(pad8(row)), stacked(b), (((1,), (1,)), ((), ())), preferred_element_type=F32
    )
    return both_halves(out[:8] + out[8:])[:1]


def eye():
    rows = lax.broadcasted_iota(jnp.int32, (H, H), 0)
    cols = lax.broadcasted_iota(jnp.int32, (H, H), 1)
    return (rows == cols).astype(F32)


def gates(proj, rec, prev):
    reset = jax.nn.sigmoid(proj[0] + rec[0])
    write = jax.nn.sigmoid(proj[1] + rec[1])
    cand = jnp.tanh(proj[2] + reset * rec[2])
    slope = write * (1.0 - cand * cand)
    terms = (
        slope * rec[2] * reset * (1.0 - reset),
        (cand - prev) * write * (1.0 - write),
        slope * reset,
    )
    off = write * cand - (terms[0] * rec[0] + terms[1] * rec[1] + terms[2] * rec[2])
    return write, terms, off


def parts3(x):
    return x[:, :H], x[:, H : 2 * H], x[:, 2 * H :]


def leaf(u, write, terms, ident):
    return u[0] * terms[0] + u[1] * terms[1] + u[2] * terms[2] - ident * write


def compose(early, late):
    lb, lv, lc = early
    rb, rv, rc = late
    prod = mm(jnp.concatenate([lb, pad8(lv)], axis=0), rb)
    return (
        lb + rb + prod[:H],
        lv + rv + prod[H : H + 1],
        lc + rc + vec_mm_t(rc, lb),
    )


def local_kernel(
    x_hbm,
    traj_hbm,
    cot_hbm,
    init_hbm,
    win_hbm,
    wrec_hbm,
    bias_hbm,
    pack_ref,
    nodes_ref,
    steps_hbm,
    x_ref,
    traj_ref,
    cot_ref,
    init_ref,
    win_ref,
    wrec_ref,
    bias_ref,
    steps_ref,
    pairs_ref,
    quads_ref,
    sems,
):
    copies = [
        pltpu.make_async_copy(src, dst, sems.at[i])
        for i, (src, dst) in enumerate(
            (
                (traj_hbm, traj_ref),
                (wrec_hbm, wrec_ref),
                (init_hbm, init_ref),
                (x_hbm, x_ref),
                (win_hbm, win_ref),
                (bias_hbm, bias_ref),
                (cot_hbm, cot_ref),
            )
        )
    ]
    for copy in copies:
        copy.start()
    for copy in copies[:3]:
        copy.wait()
    traj = traj_ref[0]
    rec_in = jnp.concatenate([traj, pad8(init_ref[...])], axis=0)
    u_side, u_back = weights_of(wrec_ref)
    rec_all = few_rows(rec_in, u_side)
    rec_init = rec_all[H : H + 1]
    rec_rows = rec_all[:H]
    for copy in copies[3:6]:
        copy.wait()
    proj = (
        jnp.dot(x_ref[0], win_ref[...], precision=lax.Precision.HIGHEST, preferred_element_type=F32)
        + bias_ref[...].reshape(1, 3 * H)
    )
    rec = pltpu.roll(rec_rows, 1, 0)
    prev = pltpu.roll(traj, 1, 0)
    write, terms, off = gates(parts3(proj), parts3(rec), prev)
    inner = lax.broadcasted_iota(jnp.int32, (H, H), 0) > 0
    write = jnp.where(inner, write, 0.0)
    terms = [jnp.where(inner, t, 0.0) for t in terms]
    off = jnp.where(inner, off, 0.0)
    for p, rows in enumerate((*terms, write, off)):
        steps_ref[p] = rows
    save = pltpu.make_async_copy(steps_ref, steps_hbm, sems.at[7])
    save.start()
    copies[6].wait()

    ident = eye()
    per_block = H // BLOCKS

    def some_pairs(k, carry):
        fwd, bwd = carry
        base = pl.multiple_of(k * 16, 16)
        for half in range(2):
            rows = [steps_ref[p, pl.ds(base + 8 * half, 8), :] for p in range(4)]
            u = [wrec_ref[:, p * H : (p + 1) * H] for p in range(3)]
            for i in range(4):
                maps = []
                for l in (2 * i, 2 * i + 1):
                    row = [r[l : l + 1] for r in rows]
                    maps.append(leaf(u, row[3], row[:3], ident))
                pairs_ref[8 * k + 4 * half + i] = maps[0] + maps[1] + mm(*maps)
        fwd = forward_step(fwd, steps_ref, k, u_side, per_block)
        _, bwd = backward_step(bwd, steps_ref, cot_ref, per_block - 1 - k, u_back, per_block)
        return fwd, bwd

    zero = jnp.zeros((BLOCKS, H), F32)
    fwd, bwd = lax.fori_loop(0, 8, some_pairs, (zero, zero), unroll=8)
    for k in range(BLOCKS):
        nodes_ref[BLOCKS + k, H:] = two_rows(fwd[k : k + 1], bwd[k : k + 1])

    def joined(ref, i):
        early, late = ref[2 * i], ref[2 * i + 1]
        return early + late + mm(early, late)

    def some_quads(k, carry):
        for i in range(8):
            quads_ref[8 * k + i] = joined(pairs_ref, 8 * k + i)
        return carry

    lax.fori_loop(0, 4, some_quads, 0, unroll=4)

    def some_blocks(k, carry):
        for i in range(8):
            nodes_ref[BLOCKS + 8 * k + i, :H] = joined(quads_ref, 8 * k + i)
        return carry

    lax.fori_loop(0, 2, some_blocks, 0, unroll=2)

    def node(n):
        return nodes_ref[n, :H], nodes_ref[n, H : H + 1], nodes_ref[n, H + 1 : H + 2]

    for n in range(BLOCKS - 1, 0, -1):
        m, v, c = compose(node(2 * n), node(2 * n + 1))
        nodes_ref[n, :H] = m
        nodes_ref[n, H:] = two_rows(v, c)
    nodes_ref[0, :8] = jnp.concatenate(
        [*parts3(rec_init), init_ref[...], jnp.zeros((4, H), F32)], axis=0
    )
    nodes_ref[0, 8:] = jnp.zeros((H, H), F32)
    m, v, c = node(1)
    rec_last = rec_rows[H - 1 : H]
    write_pack(
        pack_ref,
        m,
        [v, c]
        + [proj[0:1, p * H : (p + 1) * H] for p in range(3)]
        + [rec_last[:, p * H : (p + 1) * H] for p in range(3)]
        + [traj[H - 1 : H]],
    )
    save.wait()


def two_rows(v, c):
    return jnp.concatenate([v, c, jnp.zeros((6, H), F32)], axis=0)


def write_pack(pack_ref, m, rows):
    tail = jnp.concatenate(rows + [jnp.zeros((ROWS - H - len(rows), H), F32)], axis=0)
    for i in range(pack_ref.shape[0]):
        pack_ref[i, :H] = m
        pack_ref[i, H:] = tail


def weights_of(wrec_ref):
    u = wrec_ref[...]
    return halves(u), halves(u.T)


def every(ref, l, per_block):
    return ref[pl.ds(l, BLOCKS, stride=per_block), :]


def forward_step(h, steps_ref, l, u_side, per_block):
    term = [every(steps_ref.at[p], l, per_block) for p in range(5)]
    mapped = parts3(few_rows(h, u_side))
    moved = term[0] * mapped[0] + term[1] * mapped[1] + term[2] * mapped[2]
    return h + (moved - term[3] * h) + term[4]


def backward_step(carried, steps_ref, cot_ref, l, u_back, per_block):
    term = [every(steps_ref.at[p], l, per_block) for p in range(4)]
    costate = carried + every(cot_ref.at[0], l, per_block)
    scaled = jnp.concatenate([term[p] * costate for p in range(3)], axis=1)
    back = few_rows(scaled, u_back)
    return costate, costate + (back - term[3] * costate)


def boundaries(group_ref, wrec_ref, ident):
    u = [wrec_ref[:, p * H : (p + 1) * H] for p in range(3)]
    found = []
    for j in range(1, 4):
        proj = [group_ref[j, ROW_PROJ + p : ROW_PROJ + p + 1] for p in range(3)]
        rec = [group_ref[j - 1, ROW_REC + p : ROW_REC + p + 1] for p in range(3)]
        write, terms, off = gates(proj, rec, group_ref[j - 1, ROW_LAST : ROW_LAST + 1])
        found.append((leaf(u, write, terms, ident), off))
    return found


def links(group_ref, wrec_ref):
    ident = eye()
    firsts = boundaries(group_ref, wrec_ref, ident)
    ahead, behind = [], []
    for j in range(3):
        first, off = firsts[j]
        part = group_ref[j, :H]
        prod = mm(group_ref[j, : H + 8], first)
        ahead.append(
            (
                part + first + prod[:H],
                group_ref[j, ROW_B : ROW_B + 1] + off + prod[ROW_B : ROW_B + 1],
            )
        )
        part = group_ref[j + 1, :H]
        cc = group_ref[j + 1, ROW_C : ROW_C + 1]
        prod = mm(jnp.concatenate([first, pad8(off)], axis=0), part)
        behind.append(
            (
                part + first + prod[:H],
                off + prod[H : H + 1] + group_ref[j + 1, ROW_B : ROW_B + 1],
                cc + vec_mm_t(cc, first),
            )
        )
    return ahead, behind


def merge_kernel(group_ref, wrec_ref, pack_ref, path_ref):
    ahead, behind = links(group_ref, wrec_ref)
    put_path(path_ref, *paths_to(places()[1], ahead, [(m, c) for m, _, c in behind]))
    start = (
        group_ref[0, :H],
        group_ref[0, ROW_B : ROW_B + 1],
        group_ref[0, ROW_C : ROW_C + 1],
    )
    m, v, c = compose(compose(start, behind[0]), compose(behind[1], behind[2]))
    write_pack(
        pack_ref,
        m,
        [v, c]
        + [group_ref[0, ROW_PROJ + p : ROW_PROJ + p + 1] for p in range(3)]
        + [group_ref[3, ROW_REC + p : ROW_REC + p + 1] for p in range(3)]
        + [group_ref[3, ROW_LAST : ROW_LAST + 1]],
    )


def places():
    place = lax.axis_index("seq")
    return place // 16, place % 4


def forward_join(early, late):
    prod = mm(jnp.concatenate([early[0], pad8(early[1])], axis=0), late[0])
    return early[0] + late[0] + prod[:H], early[1] + late[1] + prod[H : H + 1]


def adjoint_join(early, late):
    return (
        early[0] + late[0] + mm(early[0], late[0]),
        early[1] + late[1] + vec_mm_t(late[1], early[0]),
    )


def paths_to(own, ahead, behind):
    keep = lambda on, new, old: tuple(jnp.where(on, n, o) for n, o in zip(new, old))
    none = (jnp.zeros((H, H), F32), jnp.zeros((1, H), F32))
    to = keep(own > 0, ahead[0], none)
    back = keep(own < 3, behind[2], none)
    for j in (1, 2):
        to = keep(own > j, forward_join(to, ahead[j]), to)
        back = keep(own < 3 - j, adjoint_join(behind[2 - j], back), back)
    return to, back


def put_path(path_ref, to, back):
    for i, (m, v) in enumerate((to, back)):
        path_ref[i, :H] = m
        path_ref[i, H:] = pad8(v)


def pair_kernel(own_ref, other_ref, inner_ref, wrec_ref, pack_ref, path_ref, *, bit):
    second = lax.axis_index("seq") // bit % 2 == 1
    own, other = own_ref[0], other_ref[0]
    early = jnp.where(second, other, own)
    late = jnp.where(second, own, other)
    u = [wrec_ref[:, p * H : (p + 1) * H] for p in range(3)]
    write, terms, off = gates(
        [late[ROW_PROJ + p : ROW_PROJ + p + 1] for p in range(3)],
        [early[ROW_REC + p : ROW_REC + p + 1] for p in range(3)],
        early[ROW_LAST : ROW_LAST + 1],
    )
    first = leaf(u, write, terms, eye())
    early_v, early_c = early[ROW_B : ROW_B + 1], early[ROW_C : ROW_C + 1]
    late_v, late_c = late[ROW_B : ROW_B + 1], late[ROW_C : ROW_C + 1]
    ahead = forward_join((early[:H], early_v), (first, off))
    prod = mm(jnp.concatenate([first, pad8(off)], axis=0), late[:H])
    behind = (
        first + late[:H] + prod[:H],
        off + prod[H : H + 1] + late_v,
        late_c + vec_mm_t(late_c, first),
    )
    to = tuple(jnp.where(second, a, 0.0) for a in ahead)
    back = tuple(jnp.where(second, 0.0, a) for a in (behind[0], behind[2]))
    put_path(
        path_ref,
        forward_join(to, (inner_ref[0, :H], inner_ref[0, H : H + 1])),
        adjoint_join((inner_ref[1, :H], inner_ref[1, H : H + 1]), back),
    )
    m, v, c = compose((early[:H], early_v, early_c), behind)
    write_pack(
        pack_ref,
        m,
        [v, c]
        + [early[ROW_PROJ + p : ROW_PROJ + p + 1] for p in range(3)]
        + [late[ROW_REC + p : ROW_REC + p + 1] for p in range(3)]
        + [late[ROW_LAST : ROW_LAST + 1]],
    )


def apply_kernel(
    group_ref,
    path_ref,
    nodes_ref,
    wrec_ref,
    steps_hbm,
    cot_hbm,
    state_ref,
    adjoint_ref,
    steps_ref,
    cot_ref,
    sems,
):
    copies = [
        pltpu.make_async_copy(steps_hbm, steps_ref, sems.at[0]),
        pltpu.make_async_copy(cot_hbm, cot_ref, sems.at[1]),
    ]
    for copy in copies:
        copy.start()
    per_block = H // BLOCKS
    ahead, behind = links(group_ref, wrec_ref)
    init = nodes_ref[0, 3:4]
    rec = [nodes_ref[0, p : p + 1] for p in range(3)]
    write, terms, off = gates(
        [group_ref[0, ROW_PROJ + p : ROW_PROJ + p + 1] for p in range(3)], rec, init
    )
    state = (
        init
        + (terms[0] * rec[0] + terms[1] * rec[1] + terms[2] * rec[2])
        - write * init
        + off
    )
    costate = jnp.zeros((1, H), F32)
    own = places()[0]
    for j in range(3):
        moved = state + vec_mm(state, ahead[j][0]) + ahead[j][1]
        state = jnp.where(j < own, moved, state)
        i = 2 - j
        moved = costate + vec_mm(costate, behind[i][0].T) + behind[i][2]
        costate = jnp.where(i >= own, moved, costate)
    states = {1: state + vec_mm(state, path_ref[0, :H]) + path_ref[0, H : H + 1]}
    costates = {1: costate + vec_mm(costate, path_ref[1, :H].T) + path_ref[1, H : H + 1]}
    for n in range(1, BLOCKS):
        state, costate = states[n], costates[n]
        states[2 * n] = state
        states[2 * n + 1] = (
            state + vec_mm(state, nodes_ref[2 * n, :H]) + nodes_ref[2 * n, H : H + 1]
        )
        costates[2 * n] = (
            costate
            + vec_mm(costate, nodes_ref[2 * n + 1, :H].T)
            + nodes_ref[2 * n + 1, H + 1 : H + 2]
        )
        costates[2 * n + 1] = costate
    fwd = jnp.concatenate([states[BLOCKS + k] for k in range(BLOCKS)], axis=0)
    bwd = jnp.concatenate([costates[BLOCKS + k] for k in range(BLOCKS)], axis=0)
    for copy in copies:
        copy.wait()
    u_side, u_back = weights_of(wrec_ref)
    for l in range(per_block):
        fwd = forward_step(fwd, steps_ref, l, u_side, per_block)
        state_ref.at[0][pl.ds(l, BLOCKS, stride=per_block), :] = fwd
        back = per_block - 1 - l
        out, bwd = backward_step(bwd, steps_ref, cot_ref, back, u_back, per_block)
        adjoint_ref.at[0][pl.ds(back, BLOCKS, stride=per_block), :] = out


def call(kernel, out_shape, flops, spaces, outs, scratch=()):
    kinds = {"s": pltpu.SMEM, "v": pltpu.VMEM, "h": pltpu.HBM}
    run = pl.pallas_call(
        kernel,
        out_shape=tuple(
            pltpu.HBM(o.shape, o.dtype) if k == "h" else o for k, o in zip(outs, out_shape)
        ),
        in_specs=[pl.BlockSpec(memory_space=kinds[k]) for k in spaces],
        out_specs=tuple(pl.BlockSpec(memory_space=kinds[k]) for k in outs),
        scratch_shapes=list(scratch),
        compiler_params=pltpu.CompilerParams(vmem_limit_bytes=VMEM_LIMIT),
        cost_estimate=pl.CostEstimate(flops=flops, bytes_accessed=2**20, transcendentals=0),
    )

    def placed(*args):
        return run(
            *(
                pltpu.with_memory_space_constraint(a, pltpu.HBM) if k == "h" else a
                for k, a in zip(spaces, args)
            )
        )

    return placed


def group_lists(count):
    near = [list(range(s, s + 4)) for s in range(0, count, 4)]
    far = [[16 * y + z for y in range(4)] for z in range(16)]
    return near, far


def shape(*dims):
    return jax.ShapeDtypeStruct(dims, F32)


def per_device(
    inputs, trajectory, initial_state, cotangent, in_weight, recurrent_weight, gate_bias
):
    count = lax.axis_size("seq")
    near, far = group_lists(count)
    pack, nodes, steps = call(
        local_kernel,
        (
            shape(4, ROWS, H),
            shape(2 * BLOCKS, H + 8, H),
            shape(5, H, H),
        ),
        2 * 10**9,
        "hhhhhhh",
        "vvh",
        [
            pltpu.VMEM((1, H, H), F32),
            pltpu.VMEM((1, H, H), F32),
            pltpu.VMEM((1, H, H), F32),
            pltpu.VMEM((1, H), F32),
            pltpu.VMEM((H, 3 * H), F32),
            pltpu.VMEM((H, 3 * H), F32),
            pltpu.VMEM((3 * H,), F32),
            pltpu.VMEM((5, H, H), F32),
            pltpu.VMEM((64, H, H), F32),
            pltpu.VMEM((32, H, H), F32),
            pltpu.SemaphoreType.DMA((8,)),
        ],
    )(
        inputs,
        trajectory,
        cotangent,
        initial_state,
        in_weight,
        recurrent_weight,
        gate_bias,
    )
    merge = call(
        merge_kernel, (shape(1, ROWS, H), shape(2, H + 8, H)), 10**8, "vv", "vv"
    )

    def exchange(packed, groups):
        return lax.all_to_all(packed, "seq", 0, 0, axis_index_groups=groups)

    def pair(packed, path, bit, flip, copies):
        other = lax.ppermute(packed, "seq", [(i, i ^ flip) for i in range(count)])
        return call(
            functools.partial(pair_kernel, bit=bit),
            (shape(copies, ROWS, H), shape(2, H + 8, H)),
            10**8,
            "vvvv",
            "vv",
        )(packed, other, path, recurrent_weight)

    pack, path = merge(exchange(pack, near), recurrent_weight)
    pack, path = pair(pack, path, 4, 7, 1)
    pack, path = pair(pack, path, 8, 12, 4)
    new_state, adjoint = call(
        apply_kernel,
        (shape(1, H, H), shape(1, H, H)),
        10**8,
        "vvvvhh",
        "vv",
        [
            pltpu.VMEM((5, H, H), F32),
            pltpu.VMEM((1, H, H), F32),
            pltpu.SemaphoreType.DMA((2,)),
        ],
    )(exchange(pack, far), path, nodes, recurrent_weight, steps, cotangent)
    return new_state, adjoint


def solution(mesh):
    return jax.shard_map(
        per_device,
        mesh=mesh,
        in_specs=(
            P("dp", "seq", None),
            P("dp", "seq", None),
            P("dp", None),
            P("dp", "seq", None),
            P(),
            P(),
            P(),
        ),
        out_specs=(P("dp", "seq", None), P("dp", "seq", None)),
        check_vma=False,
    )
```
